32 devices in a mesh: rep: 2 (over y), gx: 4 (over z), gy: 4 (over x, core).
Axes of the slice: x: 2, y: 2, z: 4, core: 2. Of those that a mesh axis runs over, the one named last changes fastest.
Arguments:
- positions: float32 [3, 8, 4, 1024], P(None, ('rep', 'gx'), 'gy'), parts along dimension 1, may hold values from 0 to 256, as said below
- charges: float32 [8, 4, 1024], P(('rep', 'gx'), 'gy'), parts along dimension 0, may hold values from -2 to 2
- pair_lists: int32 [8, 4, 4, 4], P(('rep', 'gx'), 'gy'), parts along dimension 0, may hold values from 0 to 35, as said below
- slab_dest: int32 [8, 4, 8], P(('rep', 'gx'), 'gy'), parts along dimension 0, may hold values from 0 to 3, as said below
- atom_counts: int32 [8, 4], P(('rep', 'gx'), 'gy'), parts along dimension 0, may hold values from 512 to 1024, as said below
Outputs:
- short_forces: float32 [3, 8, 4, 1024], P(None, ('rep', 'gx'), 'gy'), parts along dimension 1
- long_forces: float32 [3, 8, 4, 1024], P(None, ('rep', 'gx'), 'gy'), parts along dimension 1
The draws below stay inside these ranges and needn't reach their ends.
There are 2 independent parts, one for each index of `rep`. The reference program is written for one: setup_inputs(seed, part) draws one part's arguments, and reference() takes and returns one part's arrays. A program takes and returns all parts, laid end to end along the dimension named above; each array names one. Nothing has to cross between parts.
Inputs may be any that keep to these rules, and one draw needn't show every extreme that they name: `positions`: the first coordinate lies in [0, 64), the second in [0, 64), and the third in the slab of the atom's block, [s * 32, (s + 1) * 32). `pair_lists`: each list names 4 different clusters of the neighbourhood, the cluster's own, 16 + c for cluster c, first; the others are clusters whose blocks' slabs lie nearest to those of the cluster's own blocks. `slab_dest`: the blocks of a cell name slabs in non-decreasing order; at most 4 blocks of one cell name one slab, and in every cell some slab is named by exactly 4. `atom_counts`: some cell holds 1024 atoms in every draw.
All inputs are finite; a program needn't handle non-finite values.
Results may differ from the reference program's by a relative error of at most 0.0003.
Values sent between devices are 32-bit elements; how exact they have to be, the bound alone decides.
A program may use at most 128 MiB of HBM per device.

```python
import jax
import jax.numpy as jnp
from jax import lax

GRID_X = 256
GRID_Y = 256
GRID_Z = 128
BLOCK = 128
JLIST = 4
CLUSTERS_DEV = 4
ATOMS_DEV = 1024
BLOCKS_DEV = 8
SLOTS = 4
XC = 64
YC = 64
ZC = 32
N_GX = 4
N_GY = 4


def slab_layout(key):
    devices = N_GX * N_GY
    tokens = N_GY * SLOTS
    token_slab = jnp.arange(tokens, dtype=jnp.int32) // SLOTS

    def one_cell(cell_key):
        keys = jax.random.split(cell_key, 3)
        favour = jax.random.randint(keys[0], (N_GY,), 0, 400)
        busiest = jax.random.randint(keys[1], (), 0, N_GY)
        noise = jax.random.randint(keys[2], (tokens,), 0, 1000)
        score = noise + favour[token_slab] + 100000 * (token_slab == busiest).astype(jnp.int32)
        score = score * 4096 + jnp.arange(tokens, dtype=jnp.int32)
        picked = lax.top_k(score, BLOCKS_DEV)[1]
        return jnp.sort(token_slab[picked])
    keys = jax.random.split(jax.random.fold_in(key, 11), devices)
    return jax.vmap(one_cell)(keys).reshape(N_GX, N_GY, BLOCKS_DEV).astype(jnp.int32)


def draw_slab_dest(key, part):
    return slab_layout(key)


def draw_positions(key, part):
    slabs = slab_layout(key)
    atom_slab = jnp.repeat(slabs, BLOCK, axis=2).astype(jnp.float32)
    keys = jax.random.split(jax.random.fold_in(key, 23), 3)
    shape = (N_GX, N_GY, ATOMS_DEV)
    across = jax.random.uniform(keys[0], shape, jnp.float32, 0.0, XC * 1.0)
    along = jax.random.uniform(keys[1], shape, jnp.float32, 0.0, YC * 1.0)
    height = (atom_slab + jax.random.uniform(keys[2], shape, jnp.float32, 0.02, 0.98)) * ZC
    return jnp.stack([across, along, height])


def draw_charges(key, part):
    shape = (N_GX, N_GY, ATOMS_DEV)
    charge_key = jax.random.fold_in(key, 37)
    return jnp.clip(0.5 * jax.random.normal(charge_key, shape, jnp.float32), -2.0, 2.0)


def draw_pair_lists(key, part):
    candidates = 9 * CLUSTERS_DEV
    per_cluster = BLOCKS_DEV // CLUSTERS_DEV
    slabs = slab_layout(key).reshape(N_GX, N_GY, CLUSTERS_DEV, per_cluster)
    lowest = slabs[:, :, :, 0]
    highest = slabs[:, :, :, per_cluster - 1]
    low_parts = []
    high_parts = []
    for step_x in (-1, 0, 1):
        for step_y in (-1, 0, 1):
            low_parts.append(jnp.roll(lowest, (-step_x, -step_y), axis=(0, 1)))
            high_parts.append(jnp.roll(highest, (-step_x, -step_y), axis=(0, 1)))
    near_low = jnp.stack(low_parts, axis=2).reshape(N_GX, N_GY, candidates)
    near_high = jnp.stack(high_parts, axis=2).reshape(N_GX, N_GY, candidates)
    above = near_low[:, :, None, :] - highest[:, :, :, None]
    below = lowest[:, :, :, None] - near_high[:, :, None, :]
    slab_gap = jnp.maximum(0, jnp.maximum(above, below))
    noise = jax.random.randint(jax.random.fold_in(key, 53), (N_GX, N_GY, CLUSTERS_DEV, candidates), 0, 4096)
    own_index = 4 * CLUSTERS_DEV + jnp.arange(CLUSTERS_DEV, dtype=jnp.int32)[:, None]
    choice_index = jnp.arange(candidates, dtype=jnp.int32)[None, :]
    score = ((256 - slab_gap) * 4096 + noise) * 512 + choice_index
    score = score + (choice_index == own_index).astype(jnp.int32) * (1 << 29)
    return lax.top_k(score, JLIST)[1].astype(jnp.int32)


def draw_atom_counts(key, part):
    keys = jax.random.split(jax.random.fold_in(key, 41), 2)
    counts = jax.random.randint(keys[0], (N_GX * N_GY,), ATOMS_DEV // 2, ATOMS_DEV + 1)
    fullest = jax.random.randint(keys[1], (), 0, N_GX * N_GY)
    counts = jnp.where(jnp.arange(N_GX * N_GY) == fullest, ATOMS_DEV, counts)
    return counts.reshape(N_GX, N_GY).astype(jnp.int32)


def setup_inputs(seed: int = 0, part: int = 0) -> dict:
    key_of = jax.random.split(jax.random.key(seed), 6)
    own_keys = jax.random.split(jax.random.fold_in(key_of[5], part), 6)
    positions = draw_positions(jax.random.fold_in(jax.random.fold_in(key_of[5], part), 71), part)
    charges = draw_charges(jax.random.fold_in(jax.random.fold_in(key_of[5], part), 71), part)
    pair_lists = draw_pair_lists(jax.random.fold_in(jax.random.fold_in(key_of[5], part), 71), part)
    slab_dest = draw_slab_dest(jax.random.fold_in(jax.random.fold_in(key_of[5], part), 71), part)
    atom_counts = draw_atom_counts(jax.random.fold_in(jax.random.fold_in(key_of[5], part), 71), part)
    return dict(positions=positions, charges=charges, pair_lists=pair_lists, slab_dest=slab_dest, atom_counts=atom_counts)


spacing = 0.16
ewald_split = 3.47
cutoff = 0.9
soft_core = 0.09
root_factor = 1.1283791670955126

def spline_weights(fraction):
    remain = 1.0 - fraction
    square = fraction * fraction
    cube_part = square * fraction
    values = jnp.stack([remain * remain * remain / 6.0, (3.0 * cube_part - 6.0 * square + 4.0) / 6.0, (-3.0 * cube_part + 3.0 * square + 3.0 * fraction + 1.0) / 6.0, cube_part / 6.0])
    slopes = jnp.stack([-0.5 * remain * remain, 0.5 * (3.0 * square - 4.0 * fraction), 0.5 * (-3.0 * square + 2.0 * fraction + 1.0), 0.5 * square])
    return (values, slopes)

def split_cells(coordinate, offset, cell_count):
    inside = coordinate - offset
    lowest = jnp.clip(jnp.floor(inside).astype(jnp.int32), 0, cell_count - 1)
    return (lowest, inside - lowest.astype(inside.dtype))

def influence(index_x, index_y, index_z):

    def signed(index, period):
        return jnp.where(index <= period // 2, index, index - period).astype(jnp.float32) / (period * spacing)

    def modulus(index, period):
        return ((2.0 + jnp.cos(index.astype(jnp.float32) * (2.0 * jnp.pi / period))) / 3.0) ** 2
    wave = signed(index_x, GRID_X) ** 2 + signed(index_y, GRID_Y) ** 2 + signed(index_z, GRID_Z) ** 2
    safe_wave = jnp.where(wave > 0.0, wave, 1.0)
    volume = GRID_X * GRID_Y * GRID_Z * spacing ** 3
    green = jnp.exp(-(jnp.pi / ewald_split) ** 2 * safe_wave) / (jnp.pi * volume * safe_wave)
    green = green / (modulus(index_x, GRID_X) * modulus(index_y, GRID_Y) * modulus(index_z, GRID_Z))
    return jnp.where(wave > 0.0, green, 0.0)

def cluster_forces(own_atoms, beside_all, pair_list):

    def one_cluster(inputs):
        own_rows, chosen = inputs
        partner = beside_all[:, chosen]
        offsets = (own_rows[:3, None, :, None] - partner[:3, :, None, :]) * spacing
        dist_square = lax.optimization_barrier(jnp.sum(offsets * offsets, axis=0))
        soft_square = dist_square + soft_core
        soft_dist = jnp.sqrt(soft_square)
        scaled = ewald_split * soft_dist
        strength = (jax.scipy.special.erfc(scaled) / soft_dist + ewald_split * root_factor * jnp.exp(-scaled * scaled)) / soft_square
        cutoff_taper = jnp.where(dist_square < cutoff * cutoff, (1.0 - dist_square / (cutoff * cutoff)) ** 2, 0.0)
        weight = partner[3][:, None, :] * strength * cutoff_taper
        return own_rows[3] * lax.optimization_barrier(jnp.sum(weight[None] * offsets, axis=(1, 3)))
    return lax.map(one_cluster, (jnp.moveaxis(own_atoms, 1, 0), pair_list))

def short_range(positions, charge, pair_lists):
    count_x, count_y, atom_total = charge.shape
    clusters = pair_lists.shape[2]
    cluster_size = atom_total // clusters
    cells_x = GRID_X // count_x
    cells_y = GRID_Y // count_y
    packed = jnp.concatenate([positions, charge[None]], axis=0)
    pieces = []
    for step_x in (-1, 0, 1):
        for step_y in (-1, 0, 1):
            moved = jnp.roll(packed, (-step_x, -step_y), axis=(1, 2))
            cell_shift = jnp.array([step_x * cells_x, step_y * cells_y, 0.0, 0.0], jnp.float32)
            pieces.append(moved + cell_shift[:, None, None, None])
    devices = count_x * count_y
    beside_all = jnp.stack(pieces, axis=3).reshape(4, devices, 9 * clusters, cluster_size)
    own_atoms = packed.reshape(4, devices, clusters, cluster_size)
    listing = pair_lists.reshape(devices, clusters, pair_lists.shape[3])

    def one_cell(inputs):
        return cluster_forces(inputs[0], inputs[1], inputs[2])
    result = lax.map(one_cell, (jnp.moveaxis(own_atoms, 1, 0), jnp.moveaxis(beside_all, 1, 0), listing))
    return jnp.moveaxis(result, 2, 0).reshape(3, count_x, count_y, atom_total)

def long_range(positions, charge, slab_dest):
    count_x, count_y, atom_total = charge.shape
    cells_x = GRID_X // count_x
    cells_y = GRID_Y // count_y
    cells_z = GRID_Z // count_y
    block_size = atom_total // slab_dest.shape[2]
    slab_of = jnp.repeat(slab_dest, block_size, axis=2)
    column_x = jnp.arange(count_x, dtype=jnp.int32)[:, None, None]
    column_y = jnp.arange(count_y, dtype=jnp.int32)[None, :, None]
    lowest_x, fraction_x = split_cells(positions[0], 0.0, cells_x)
    lowest_y, fraction_y = split_cells(positions[1], 0.0, cells_y)
    lowest_z, fraction_z = split_cells(positions[2], (slab_of * cells_z).astype(jnp.float32), cells_z)
    point_x = column_x * cells_x + lowest_x
    point_y = column_y * cells_y + lowest_y
    point_z = slab_of * cells_z + lowest_z
    values_x, slopes_x = spline_weights(fraction_x)
    values_y, slopes_y = spline_weights(fraction_y)
    values_z, slopes_z = spline_weights(fraction_z)
    charge_mesh = jnp.zeros((GRID_X, GRID_Y, GRID_Z), jnp.float32)
    for term_x in range(4):
        for term_y in range(4):
            for term_z in range(4):
                charge_mesh = charge_mesh.at[(point_x + term_x) % GRID_X, (point_y + term_y) % GRID_Y, (point_z + term_z) % GRID_Z].add(charge * values_x[term_x] * values_y[term_y] * values_z[term_z])
    green = influence(jnp.arange(GRID_X, dtype=jnp.int32)[:, None, None], jnp.arange(GRID_Y, dtype=jnp.int32)[None, :, None], jnp.arange(GRID_Z, dtype=jnp.int32)[None, None, :])
    potential = jnp.real(jnp.fft.ifftn(green * jnp.fft.fftn(charge_mesh))) * (GRID_X * GRID_Y * GRID_Z)
    force_x = jnp.zeros_like(charge)
    force_y = jnp.zeros_like(charge)
    force_z = jnp.zeros_like(charge)
    for term_x in range(4):
        for term_y in range(4):
            for term_z in range(4):
                sample = potential[(point_x + term_x) % GRID_X, (point_y + term_y) % GRID_Y, (point_z + term_z) % GRID_Z]
                force_x = force_x + slopes_x[term_x] * values_y[term_y] * values_z[term_z] * sample
                force_y = force_y + values_x[term_x] * slopes_y[term_y] * values_z[term_z] * sample
                force_z = force_z + values_x[term_x] * values_y[term_y] * slopes_z[term_z] * sample
    factor = -charge / spacing
    return jnp.stack([factor * force_x, factor * force_y, factor * force_z])

def reference(positions, charges, pair_lists, slab_dest, atom_counts):
    living = jnp.arange(charges.shape[2], dtype=jnp.int32)[None, None, :] < atom_counts[:, :, None]
    charge = jnp.where(living, charges, 0.0)
    return (short_range(positions, charge, pair_lists), long_range(positions, charge, slab_dest))
```

```python
import functools
import math

import jax
import jax.numpy as jnp
import numpy as np
from jax import lax
from jax.experimental import pallas as pl
from jax.experimental.pallas import tpu as pltpu
from jax.sharding import PartitionSpec as P

GRID_X = 256
GRID_Y = 256
GRID_Z = 128


spacing = 0.16
ewald_split = 3.47
cutoff = 0.9
soft_core = 0.09
root_factor = 1.1283791670955126
rows_group = 8


def with_halo(value, sides, width):
    for axis, dim in sides:
        count, length = (lax.axis_size(axis), value.shape[dim])
        up = [(i, (i + 1) % count) for i in range(count)]
        down = [(j, i) for i, j in up]
        last = lax.slice_in_dim(value, length - width, length, axis=dim)
        initial = lax.slice_in_dim(value, 0, width, axis=dim)
        before = lax.ppermute(last, axis, up)
        after = lax.ppermute(initial, axis, down)
        value = jnp.concatenate([before, value, after], axis=dim)
    return value


def moved(value, step_x, step_y):
    count_x = lax.axis_size("gx")
    count_y = lax.axis_size("gy")
    pairs = [
        (i * count_y + j, (i + step_x) % count_x * count_y + (j + step_y) % count_y)
        for i in range(count_x)
        for j in range(count_y)
    ]
    return lax.ppermute(value, ("gx", "gy"), pairs)


def round_up(value, multiple):
    return -(-value // multiple) * multiple


def hartley(period):
    turns = np.outer(np.arange(period), np.arange(period)) % period
    phases = turns * (2.0 * np.pi / period)
    return (np.cos(phases) + np.sin(phases)).astype(np.float32)


def halves(value):
    high = value.astype(jnp.bfloat16)
    low = (value - high.astype(jnp.float32)).astype(jnp.bfloat16)
    return (high, low)


def dot(left_side, right_side):
    return jnp.dot(left_side, right_side, preferred_element_type=jnp.float32)


def spline_weights(fraction):
    remain = 1.0 - fraction
    square = fraction * fraction
    cube_part = square * fraction
    values = [
        remain * remain * remain / 6.0,
        (3.0 * cube_part - 6.0 * square + 4.0) / 6.0,
        (-3.0 * cube_part + 3.0 * square + 3.0 * fraction + 1.0) / 6.0,
        cube_part / 6.0,
    ]
    slopes = [
        -0.5 * remain * remain,
        0.5 * (3.0 * square - 4.0 * fraction),
        0.5 * (-3.0 * square + 2.0 * fraction + 1.0),
        0.5 * square,
    ]
    return (values, slopes)


def split_cells(coordinate, offset, cell_count):
    inside = coordinate - offset
    lowest = jnp.clip(jnp.floor(inside).astype(jnp.int32), 0, cell_count - 1)
    return (lowest, inside - lowest.astype(inside.dtype))


def spline_table(lowest, values, table_size, period=None):
    points = lax.broadcasted_iota(jnp.int32, (table_size, lowest.shape[1]), 0)
    lookup = jnp.zeros(points.shape, jnp.float32)
    for spline_term in range(4):
        at = lowest + spline_term
        if period is not None:
            at = jnp.where(at >= period, at - period, at)
        lookup = jnp.where(points == at, values[spline_term], lookup)
    return lookup


def spread_kernel(cells, pad, atoms_ref, base_ref, turn_ref, out_ref, wx_ref, wy_ref, wz_ref, hi_ref, lo_ref):
    cells_x, cells_y, cells_z = cells
    pad_x, pad_y = pad
    atom_total = atoms_ref.shape[1]
    low_x, frac_x = split_cells(atoms_ref[0:1, :], 0.0, cells_x)
    low_y, frac_y = split_cells(atoms_ref[1:2, :], 0.0, cells_y)
    base = base_ref[...]
    low_z, frac_z = split_cells(atoms_ref[2:3, :], base.astype(jnp.float32), cells_z)
    wx_ref[...] = spline_table(low_x, spline_weights(frac_x)[0], pad_x) * atoms_ref[3:4, :]
    wy_ref[...] = spline_table(low_y, spline_weights(frac_y)[0], pad_y)
    turn = turn_ref[...]
    size_z = turn.shape[0]
    table_z = spline_table(base + low_z, spline_weights(frac_z)[0], size_z, size_z)
    waves = jnp.dot(
        turn, table_z, precision=lax.Precision.HIGHEST, preferred_element_type=jnp.float32
    ).T
    high, low = halves(waves)
    wz_ref[:, :size_z] = high
    wz_ref[:, size_z:] = low

    @pl.loop(0, pad_x // rows_group)
    def _(chunk):
        for inner in range(rows_group):
            row = wx_ref[pl.ds(chunk * rows_group + inner, 1), :]
            high, low = halves(row * wy_ref[...])
            hi_ref[pl.ds(inner * pad_y, pad_y), :] = high
            lo_ref[pl.ds(inner * pad_y, pad_y), :] = low
        both = dot(hi_ref[...], wz_ref[...])
        rest = dot(lo_ref[...], wz_ref[:, :size_z])
        total = both[:, :size_z] + both[:, size_z:] + rest
        out_ref[pl.ds(chunk * rows_group, rows_group)] = total.reshape(rows_group, pad_y, size_z)


def gather_kernel(cells, pad, atoms_ref, base_ref, turn_ref, mesh_ref, out_ref, wx_ref, vx_ref, wy_ref, vy_ref, wz_ref, level_ref):
    cells_x, cells_y, cells_z = cells
    pad_x, pad_y = pad
    atom_total = atoms_ref.shape[1]
    low_x, frac_x = split_cells(atoms_ref[0:1, :], 0.0, cells_x)
    low_y, frac_y = split_cells(atoms_ref[1:2, :], 0.0, cells_y)
    base = base_ref[...]
    low_z, frac_z = split_cells(atoms_ref[2:3, :], base.astype(jnp.float32), cells_z)
    values, slopes = spline_weights(frac_x)
    wx_ref[...] = spline_table(low_x, values, pad_x)
    vx_ref[...] = spline_table(low_x, slopes, pad_x)
    values, slopes = spline_weights(frac_y)
    wy_ref[...] = spline_table(low_y, values, pad_y)
    vy_ref[...] = spline_table(low_y, slopes, pad_y)
    values, slopes = spline_weights(frac_z)
    turn = turn_ref[...]
    size_z = turn.shape[0]
    for place, terms in enumerate((values, slopes)):
        table_z = spline_table(base + low_z, terms, size_z, size_z)
        waves = jnp.dot(
            turn, table_z, precision=lax.Precision.HIGHEST, preferred_element_type=jnp.float32
        )
        high, low = halves(waves)
        wz_ref[:size_z, pl.ds(place * atom_total, atom_total)] = high
        wz_ref[size_z:, pl.ds(place * atom_total, atom_total)] = low
    groups = pad_y // 8

    def one_chunk(chunk, sums):
        rows = mesh_ref[pl.ds(chunk * rows_group, rows_group)].reshape(rows_group * pad_y, size_z)
        high, low = halves(rows)
        level_ref[...] = dot(jnp.concatenate([high, high], axis=1), wz_ref[...]) + dot(
            low, wz_ref[:size_z, :]
        )
        first, second, third = sums
        for inner in range(rows_group):
            flat = level_ref[pl.ds(inner * pad_y, pad_y), :atom_total]
            tilt = level_ref[pl.ds(inner * pad_y, pad_y), atom_total:]
            across = wy_ref[...]
            part_x = jnp.sum((across * flat).reshape(groups, 8, atom_total), axis=0)
            part_y = jnp.sum((vy_ref[...] * flat).reshape(groups, 8, atom_total), axis=0)
            part_z = jnp.sum((across * tilt).reshape(groups, 8, atom_total), axis=0)
            weight = wx_ref[pl.ds(chunk * rows_group + inner, 1), :]
            slope = vx_ref[pl.ds(chunk * rows_group + inner, 1), :]
            first = first + slope * part_x
            second = second + weight * part_y
            third = third + weight * part_z
        return (first, second, third)

    zero = jnp.zeros((8, atom_total), jnp.float32)
    sums = lax.fori_loop(0, pad_x // rows_group, one_chunk, (zero, zero, zero))
    factor = -atoms_ref[3:4, :] / spacing
    for place in range(3):
        out_ref[pl.ds(place, 1), :] = factor * jnp.sum(sums[place], axis=0, keepdims=True)


def wave_kernel(mesh_ref, xh_ref, xl_ref, yh_ref, yl_ref, column_ref, row_ref, depth_ref, out_ref):
    def across(value):
        high, low = halves(value)
        return dot(xh_ref[...], high) + dot(xl_ref[...], high) + dot(xh_ref[...], low)

    def along(value):
        high, low = halves(value)
        return dot(high, yh_ref[...]) + dot(high, yl_ref[...]) + dot(low, yh_ref[...])

    waves = along(across(mesh_ref[0]))
    square = column_ref[:, 0:1] + row_ref[0:1, :] + depth_ref[0, 0:1, 0:1]
    scale = column_ref[:, 1:2] * row_ref[1:2, :] * depth_ref[0, 0:1, 1:2]
    green = jnp.where(square > 0.0, scale / jnp.where(square > 0.0, square, 1.0), 0.0)
    out_ref[0] = across(along(waves * green))


def green_factors(index, period):
    signed = jnp.where(index <= period // 2, index, index - period).astype(jnp.float32) / (
        period * spacing
    )
    modulus = ((2.0 + jnp.cos(index.astype(jnp.float32) * (2.0 * jnp.pi / period))) / 3.0) ** 2
    square = signed * signed
    return jnp.stack([square, jnp.exp(-((jnp.pi / ewald_split) ** 2) * square) / modulus])


def one_cluster(own_rows, partner):
    offsets = (own_rows[:3, :, None] - partner[:3, None, :]) * spacing
    dist_square = jnp.sum(offsets * offsets, axis=0)
    soft_square = dist_square + soft_core
    soft_dist = jnp.sqrt(soft_square)
    scaled = ewald_split * soft_dist
    strength = (
        jax.scipy.special.erfc(scaled) / soft_dist
        + ewald_split * root_factor * jnp.exp(-scaled * scaled)
    ) / soft_square
    cutoff_taper = jnp.where(
        dist_square < cutoff * cutoff, (1.0 - dist_square / (cutoff * cutoff)) ** 2, 0.0
    )
    weight = partner[3][None, :] * strength * cutoff_taper
    return own_rows[3] * jnp.sum(weight[None] * offsets, axis=2)


def convolved_by_planes(charge_mesh, count_x, count_y):
    cells_x, cells_y = charge_mesh.shape[:2]
    devices = count_x * count_y
    place = lax.axis_index("gx") * count_y + lax.axis_index("gy")
    depth = GRID_Z // devices
    outgoing = jnp.transpose(charge_mesh.reshape(cells_x * cells_y, GRID_Z)).reshape(
        devices, depth, cells_x * cells_y
    )
    arrived = lax.all_to_all(outgoing, ("gx", "gy"), split_axis=0, concat_axis=0, tiled=True)
    planes = (
        arrived.reshape(count_x, count_y, depth, cells_x, cells_y)
        .transpose(2, 0, 3, 1, 4)
        .reshape(depth, GRID_X, GRID_Y)
    )
    turn_x = halves(jnp.asarray(hartley(GRID_X)))
    turn_y = halves(jnp.asarray(hartley(GRID_Y)))
    volume = GRID_X * GRID_Y * GRID_Z * spacing**3
    column = green_factors(jnp.arange(GRID_X, dtype=jnp.int32), GRID_X).T
    row = green_factors(jnp.arange(GRID_Y, dtype=jnp.int32), GRID_Y)
    deep = green_factors(place * depth + jnp.arange(depth, dtype=jnp.int32), GRID_Z)
    deep = (deep * jnp.array([[1.0], [1.0 / (math.pi * volume)]], jnp.float32)).T[:, None, :]

    def whole(*shape):
        return pl.BlockSpec(shape, lambda k: (0,) * len(shape))

    plane = pl.BlockSpec((1, GRID_X, GRID_Y), lambda k: (k, 0, 0))
    waves = pl.pallas_call(
        wave_kernel,
        grid=(depth,),
        in_specs=[
            plane,
            whole(GRID_X, GRID_X),
            whole(GRID_X, GRID_X),
            whole(GRID_Y, GRID_Y),
            whole(GRID_Y, GRID_Y),
            whole(GRID_X, 2),
            whole(2, GRID_Y),
            pl.BlockSpec((1, 1, 2), lambda k: (k, 0, 0)),
        ],
        out_specs=plane,
        out_shape=jax.ShapeDtypeStruct((depth, GRID_X, GRID_Y), jnp.float32),
        name="waves",
    )(planes, *turn_x, *turn_y, column, row, deep)
    outgoing = (
        waves.reshape(depth, count_x, cells_x, count_y, cells_y)
        .transpose(1, 3, 0, 2, 4)
        .reshape(devices, depth, cells_x * cells_y)
    )
    arrived = lax.all_to_all(outgoing, ("gx", "gy"), split_axis=0, concat_axis=0, tiled=True)
    return jnp.transpose(arrived.reshape(GRID_Z, cells_x * cells_y)).reshape(
        cells_x, cells_y, GRID_Z
    )


def convolved_by_lines(charge_mesh, count_x, count_y):
    turn_x = jnp.asarray(hartley(GRID_X))
    turn_y = jnp.asarray(hartley(GRID_Y))
    product = functools.partial(
        jnp.einsum, precision=lax.Precision.HIGHEST, preferred_element_type=jnp.float32
    )
    exchange = functools.partial(lax.all_to_all, tiled=True)
    lines = exchange(charge_mesh, "gx", split_axis=2, concat_axis=0)
    lines = product("xyk,xu->uyk", lines, turn_x)
    lines = exchange(lines, "gy", split_axis=0, concat_axis=1)
    lines = product("uyk,yv->uvk", lines, turn_y)
    wide, _, depth = lines.shape
    start_x = lax.axis_index("gy") * wide
    start_z = lax.axis_index("gx") * depth
    volume = GRID_X * GRID_Y * GRID_Z * spacing**3
    fx = green_factors(start_x + jnp.arange(wide, dtype=jnp.int32), GRID_X)
    fy = green_factors(jnp.arange(GRID_Y, dtype=jnp.int32), GRID_Y)
    fz = green_factors(start_z + jnp.arange(depth, dtype=jnp.int32), GRID_Z)
    square = fx[0][:, None, None] + fy[0][:, None] + fz[0]
    scale = fx[1][:, None, None] * fy[1][:, None] * fz[1] / (math.pi * volume)
    lines = lines * jnp.where(square > 0.0, scale / jnp.where(square > 0.0, square, 1.0), 0.0)
    lines = product("uvk,vy->uyk", lines, turn_y)
    lines = exchange(lines, "gy", split_axis=1, concat_axis=0)
    lines = product("uyk,ux->xyk", lines, turn_x)
    return exchange(lines, "gx", split_axis=0, concat_axis=2)


def local(positions, charges, pair_lists, slab_dest, atom_counts):
    count_x = lax.axis_size("gx")
    count_y = lax.axis_size("gy")
    devices = count_x * count_y
    atom_total = positions.shape[3]
    clusters = pair_lists.shape[2]
    cluster_size = atom_total // clusters
    blocks = slab_dest.shape[2]
    block_size = atom_total // blocks
    cells_x = GRID_X // count_x
    cells_y = GRID_Y // count_y
    cells_z = GRID_Z // count_y
    living = jnp.arange(atom_total, dtype=jnp.int32) < atom_counts[0, 0]
    charge = jnp.where(living, charges[0, 0], 0.0)
    packed = jnp.concatenate([positions, charge[None, None, None, :]], axis=0)
    atoms = packed.reshape(4, atom_total)

    base = jnp.broadcast_to(
        (slab_dest[0, 0] * cells_z)[:, None], (blocks, block_size)
    ).reshape(1, atom_total)
    cells = (cells_x, cells_y, cells_z)
    pad = (round_up(cells_x + 3, rows_group), round_up(cells_y + 3, 8))
    pad_x, pad_y = pad
    turn_z = jnp.asarray(hartley(GRID_Z))
    spread = pl.pallas_call(
        functools.partial(spread_kernel, cells, pad),
        out_shape=jax.ShapeDtypeStruct((pad_x, pad_y, GRID_Z), jnp.float32),
        scratch_shapes=[
            pltpu.VMEM((pad_x, atom_total), jnp.float32),
            pltpu.VMEM((pad_y, atom_total), jnp.float32),
            pltpu.VMEM((atom_total, 2 * GRID_Z), jnp.bfloat16),
            pltpu.VMEM((rows_group * pad_y, atom_total), jnp.bfloat16),
            pltpu.VMEM((rows_group * pad_y, atom_total), jnp.bfloat16),
        ],
        name="spread",
    )(atoms, base, turn_z)

    from_x = moved(spread[cells_x : cells_x + 3, :cells_y], 1, 0)
    from_y = moved(spread[:cells_x, cells_y : cells_y + 3], 0, 1)
    from_both = moved(spread[cells_x : cells_x + 3, cells_y : cells_y + 3], 1, 1)
    charge_mesh = (
        spread[:cells_x, :cells_y]
        .at[:3]
        .add(from_x)
        .at[:, :3]
        .add(from_y)
        .at[:3, :3]
        .add(from_both)
    )
    by_planes = GRID_Z % devices == 0
    convolved = convolved_by_planes if by_planes else convolved_by_lines
    potential = convolved(charge_mesh, count_x, count_y)
    upper_x = moved(potential[:3], -1, 0)
    upper_y = moved(potential[:, :3], 0, -1)
    upper_both = moved(potential[:3, :3], -1, -1)
    wider = jnp.concatenate(
        [
            jnp.concatenate([potential, upper_x], axis=0),
            jnp.concatenate([upper_y, upper_both], axis=0),
        ],
        axis=1,
    )
    wider = jnp.pad(wider, ((0, pad_x - cells_x - 3), (0, pad_y - cells_y - 3), (0, 0)))
    far_part = pl.pallas_call(
        functools.partial(gather_kernel, cells, pad),
        out_shape=jax.ShapeDtypeStruct((3, atom_total), jnp.float32),
        scratch_shapes=[
            pltpu.VMEM((pad_x, atom_total), jnp.float32),
            pltpu.VMEM((pad_x, atom_total), jnp.float32),
            pltpu.VMEM((pad_y, atom_total), jnp.float32),
            pltpu.VMEM((pad_y, atom_total), jnp.float32),
            pltpu.VMEM((2 * GRID_Z, 2 * atom_total), jnp.bfloat16),
            pltpu.VMEM((rows_group * pad_y, 2 * atom_total), jnp.float32),
        ],
        name="gather",
    )(atoms, base, turn_z, wider)

    nearby = with_halo(packed, (("gx", 1), ("gy", 2)), 1)
    steps_x = (jnp.arange(3, dtype=jnp.float32) - 1.0) * cells_x
    steps_y = (jnp.arange(3, dtype=jnp.float32) - 1.0) * cells_y
    zero_grid = jnp.zeros((3, 3), jnp.float32)
    cell_shift = jnp.stack(
        [steps_x[:, None] + zero_grid, steps_y[None, :] + zero_grid, zero_grid, zero_grid]
    )
    beside_all = (nearby + cell_shift[:, :, :, None]).reshape(4, 9 * clusters, cluster_size)
    chosen = pair_lists[0, 0]
    pick = (chosen[:, :, None] == jnp.arange(9 * clusters, dtype=jnp.int32)).astype(jnp.float32)
    partners = jnp.einsum(
        "cln,fnk->cflk",
        pick,
        beside_all,
        precision=lax.Precision.HIGHEST,
        preferred_element_type=jnp.float32,
    ).reshape(clusters, 4, -1)
    own = packed.reshape(4, clusters, cluster_size)
    pair_part = jnp.stack(
        [one_cluster(own[:, c], partners[c]) for c in range(clusters)], axis=1
    )
    short_forces = pair_part.reshape(3, 1, 1, atom_total)
    return (short_forces, far_part.reshape(3, 1, 1, atom_total))


def solution(mesh):
    return jax.shard_map(
        local,
        mesh=mesh,
        in_specs=(
            P(None, ("rep", "gx"), "gy", None),
            P(("rep", "gx"), "gy", None),
            P(("rep", "gx"), "gy", None, None),
            P(("rep", "gx"), "gy", None),
            P(("rep", "gx"), "gy"),
        ),
        out_specs=(P(None, ("rep", "gx"), "gy", None), P(None, ("rep", "gx"), "gy", None)),
        check_vma=False,
    )
```

```python
import functools
import math

import jax
import jax.numpy as jnp
import numpy as np
from jax import lax
from jax.experimental import pallas as pl
from jax.experimental.pallas import tpu as pltpu
from jax.sharding import PartitionSpec as P

GRID_X = 256
GRID_Y = 256
GRID_Z = 128


spacing = 0.16
ewald_split = 3.47
cutoff = 0.9
soft_core = 0.09
root_factor = 1.1283791670955126
rows_group = 8


def moved(value, step_x, step_y):
    count_x = lax.axis_size("gx")
    count_y = lax.axis_size("gy")
    pairs = [
        (i * count_y + j, (i + step_x) % count_x * count_y + (j + step_y) % count_y)
        for i in range(count_x)
        for j in range(count_y)
    ]
    return lax.ppermute(value, ("gx", "gy"), pairs)


def round_up(value, multiple):
    return -(-value // multiple) * multiple


def hartley(period):
    turns = np.outer(np.arange(period), np.arange(period)) % period
    phases = turns * (2.0 * np.pi / period)
    return (np.cos(phases) + np.sin(phases)).astype(np.float32)


def halves(value):
    high = value.astype(jnp.bfloat16)
    low = (value - high.astype(jnp.float32)).astype(jnp.bfloat16)
    return (high, low)


def dot(left_side, right_side):
    return jnp.dot(left_side, right_side, preferred_element_type=jnp.float32)


def spline_weights(fraction):
    remain = 1.0 - fraction
    square = fraction * fraction
    cube_part = square * fraction
    values = [
        remain * remain * remain / 6.0,
        (3.0 * cube_part - 6.0 * square + 4.0) / 6.0,
        (-3.0 * cube_part + 3.0 * square + 3.0 * fraction + 1.0) / 6.0,
        cube_part / 6.0,
    ]
    slopes = [
        -0.5 * remain * remain,
        0.5 * (3.0 * square - 4.0 * fraction),
        0.5 * (-3.0 * square + 2.0 * fraction + 1.0),
        0.5 * square,
    ]
    return (values, slopes)


def split_cells(coordinate, offset, cell_count):
    inside = coordinate - offset
    lowest = jnp.clip(jnp.floor(inside).astype(jnp.int32), 0, cell_count - 1)
    return (lowest, inside - lowest.astype(inside.dtype))


def spline_table(lowest, values, table_size, period=None):
    points = lax.broadcasted_iota(jnp.int32, (table_size, lowest.shape[1]), 0)
    lookup = jnp.zeros(points.shape, jnp.float32)
    for spline_term in range(4):
        at = lowest + spline_term
        if period is not None:
            at = jnp.where(at >= period, at - period, at)
        lookup = jnp.where(points == at, values[spline_term], lookup)
    return lookup


def spread_kernel(cells, pad, atoms_ref, base_ref, turn_ref, out_ref, wx_ref, wy_ref, wz_ref, hi_ref, lo_ref):
    cells_x, cells_y, cells_z = cells
    pad_x, pad_y = pad
    atom_total = atoms_ref.shape[1]
    low_x, frac_x = split_cells(atoms_ref[0:1, :], 0.0, cells_x)
    low_y, frac_y = split_cells(atoms_ref[1:2, :], 0.0, cells_y)
    base = base_ref[...]
    low_z, frac_z = split_cells(atoms_ref[2:3, :], base.astype(jnp.float32), cells_z)
    wx_ref[...] = spline_table(low_x, spline_weights(frac_x)[0], pad_x) * atoms_ref[3:4, :]
    wy_ref[...] = spline_table(low_y, spline_weights(frac_y)[0], pad_y)
    turn = turn_ref[...]
    size_z = turn.shape[0]
    table_z = spline_table(base + low_z, spline_weights(frac_z)[0], size_z, size_z)
    waves = jnp.dot(
        turn, table_z, precision=lax.Precision.HIGHEST, preferred_element_type=jnp.float32
    ).T
    high, low = halves(waves)
    wz_ref[:, :size_z] = high
    wz_ref[:, size_z:] = low

    @pl.loop(0, pad_x // rows_group)
    def _(chunk):
        for inner in range(rows_group):
            row = wx_ref[pl.ds(chunk * rows_group + inner, 1), :]
            high, low = halves(row * wy_ref[...])
            hi_ref[pl.ds(inner * pad_y, pad_y), :] = high
            lo_ref[pl.ds(inner * pad_y, pad_y), :] = low
        both = dot(hi_ref[...], wz_ref[...])
        rest = dot(lo_ref[...], wz_ref[:, :size_z])
        total = both[:, :size_z] + both[:, size_z:] + rest
        out_ref[pl.ds(chunk * rows_group, rows_group)] = total.reshape(rows_group, pad_y, size_z)


def gather_kernel(cells, pad, atoms_ref, base_ref, turn_ref, mesh_ref, out_ref, wx_ref, vx_ref, wy_ref, vy_ref, wz_ref, level_ref):
    cells_x, cells_y, cells_z = cells
    pad_x, pad_y = pad
    atom_total = atoms_ref.shape[1]
    low_x, frac_x = split_cells(atoms_ref[0:1, :], 0.0, cells_x)
    low_y, frac_y = split_cells(atoms_ref[1:2, :], 0.0, cells_y)
    base = base_ref[...]
    low_z, frac_z = split_cells(atoms_ref[2:3, :], base.astype(jnp.float32), cells_z)
    values, slopes = spline_weights(frac_x)
    wx_ref[...] = spline_table(low_x, values, pad_x)
    vx_ref[...] = spline_table(low_x, slopes, pad_x)
    values, slopes = spline_weights(frac_y)
    wy_ref[...] = spline_table(low_y, values, pad_y)
    vy_ref[...] = spline_table(low_y, slopes, pad_y)
    values, slopes = spline_weights(frac_z)
    turn = turn_ref[...]
    size_z = turn.shape[0]
    for place, terms in enumerate((values, slopes)):
        table_z = spline_table(base + low_z, terms, size_z, size_z)
        waves = jnp.dot(
            turn, table_z, precision=lax.Precision.HIGHEST, preferred_element_type=jnp.float32
        )
        high, low = halves(waves)
        wz_ref[:size_z, pl.ds(place * atom_total, atom_total)] = high
        wz_ref[size_z:, pl.ds(place * atom_total, atom_total)] = low
    groups = pad_y // 8

    def one_chunk(chunk, sums):
        rows = mesh_ref[pl.ds(chunk * rows_group, rows_group)].reshape(rows_group * pad_y, size_z)
        high, low = halves(rows)
        level_ref[...] = dot(jnp.concatenate([high, high], axis=1), wz_ref[...]) + dot(
            low, wz_ref[:size_z, :]
        )
        first, second, third = sums
        for inner in range(rows_group):
            flat = level_ref[pl.ds(inner * pad_y, pad_y), :atom_total]
            tilt = level_ref[pl.ds(inner * pad_y, pad_y), atom_total:]
            across = wy_ref[...]
            part_x = jnp.sum((across * flat).reshape(groups, 8, atom_total), axis=0)
            part_y = jnp.sum((vy_ref[...] * flat).reshape(groups, 8, atom_total), axis=0)
            part_z = jnp.sum((across * tilt).reshape(groups, 8, atom_total), axis=0)
            weight = wx_ref[pl.ds(chunk * rows_group + inner, 1), :]
            slope = vx_ref[pl.ds(chunk * rows_group + inner, 1), :]
            first = first + slope * part_x
            second = second + weight * part_y
            third = third + weight * part_z
        return (first, second, third)

    zero = jnp.zeros((8, atom_total), jnp.float32)
    sums = lax.fori_loop(0, pad_x // rows_group, one_chunk, (zero, zero, zero))
    factor = -atoms_ref[3:4, :] / spacing
    for place in range(3):
        out_ref[pl.ds(place, 1), :] = factor * jnp.sum(sums[place], axis=0, keepdims=True)


def depth_rows(table, height, fraction, terms):
    turns = (height * table[:, 0:1]).astype(jnp.int32) % GRID_Z
    phases = turns.astype(jnp.float32) * (2.0 * math.pi / GRID_Z)
    cosine, sine = (jnp.cos(phases), jnp.sin(phases))
    results = []
    for weights in terms:
        even = sum(table[:, 1 + t : 2 + t] * weights[t] for t in range(4))
        odd = sum(table[:, 5 + t : 6 + t] * weights[t] for t in range(4))
        results.append(cosine * even + sine * odd)
    return results


def mesh_kernel(sizes, cells, pad, atoms_ref, xh_ref, xl_ref, yh_ref, yl_ref, column_ref, row_ref, depth_ref, table_ref, out_ref, wx_ref, vx_ref, wy_ref, hi_ref, lo_ref, mesh_ref, turned_ref, level_ref, stack_ref, side_ref):
    count_x, count_y = sizes
    cells_x, cells_y = cells
    pad_x, pad_y = pad
    atom_total = atoms_ref.shape[2]
    depth = depth_ref.shape[0]
    window = 2 * cells_y
    windows = GRID_Y // window
    lane = lax.broadcasted_iota(jnp.int32, (depth * pad_x, window), 1)
    mesh_ref[...] = jnp.zeros_like(mesh_ref)
    wy_ref[...] = jnp.zeros_like(wy_ref)
    table = table_ref[...]

    def atoms_of(cell, row):
        return atoms_ref[cell, row : row + 1, :]

    def spread_cell(cell, i, j):
        low_x, frac_x = split_cells(atoms_of(cell, 0), 0.0, cells_x)
        low_y, frac_y = split_cells(atoms_of(cell, 1), 0.0, cells_y)
        wx_ref[...] = spline_table(low_x, spline_weights(frac_x)[0], pad_x)
        high, low = halves(spline_table(low_y, spline_weights(frac_y)[0], pad_y))
        wy_ref[:pad_y, :] = high
        wy_ref[pl.ds(window, pad_y), :] = low
        frac_z = atoms_of(cell, 5)
        (deep,) = depth_rows(table, atoms_of(cell, 4), frac_z, [spline_weights(frac_z)[0]])
        deep = deep * atoms_of(cell, 3)
        for k in range(depth):
            high, low = halves(deep[k : k + 1, :] * wx_ref[...])
            hi_ref[pl.ds(k * pad_x, pad_x), :] = high
            lo_ref[pl.ds(k * pad_x, pad_x), :] = low
        numbers = (((1,), (1,)), ((), ()))
        both = lax.dot_general(
            hi_ref[...], wy_ref[...], numbers, preferred_element_type=jnp.float32
        )
        rest = lax.dot_general(
            lo_ref[...], wy_ref[:window, :], numbers, preferred_element_type=jnp.float32
        )
        total = both[:, :window] + both[:, window:] + rest
        rows = pl.ds(pl.multiple_of(i * cells_x, 8), pad_x)
        m = j // 2
        if j % 2 == 0:
            mesh_ref[:, rows, pl.ds(m * window, window)] += total.reshape(depth, pad_x, window)
        else:
            total = pltpu.roll(total, cells_y, 1)
            kept = jnp.where(lane >= cells_y, total, 0.0)
            carried = jnp.where(lane < cells_y, total, 0.0)
            after = (m + 1) % windows
            mesh_ref[:, rows, pl.ds(m * window, window)] += kept.reshape(depth, pad_x, window)
            mesh_ref[:, rows, pl.ds(after * window, window)] += carried.reshape(
                depth, pad_x, window
            )

    @pl.loop(0, count_x)
    def _(i):
        for j in range(count_y):
            spread_cell(i * count_y + j, i, j)

    def across(value):
        high, low = halves(value)
        return dot(xh_ref[...], high) + dot(xl_ref[...], high) + dot(xh_ref[...], low)

    def along(value):
        high, low = halves(value)
        return dot(high, yh_ref[...]) + dot(high, yl_ref[...]) + dot(low, yh_ref[...])

    extra = mesh_ref.shape[1] - GRID_X

    @pl.loop(0, depth)
    def _(k):
        mesh_ref[k, :extra, :] += mesh_ref[k, GRID_X:, :]
        waves = along(across(mesh_ref[k, :GRID_X, :]))
        square = column_ref[:, 0:1] + row_ref[0:1, :] + depth_ref[k, 0:1, 0:1]
        scale = column_ref[:, 1:2] * row_ref[1:2, :] * depth_ref[k, 0:1, 1:2]
        green = jnp.where(square > 0.0, scale / jnp.where(square > 0.0, square, 1.0), 0.0)
        plane = across(along(waves * green))
        mesh_ref[k, :GRID_X, :] = plane
        mesh_ref[k, GRID_X:, :] = plane[:extra]
        rolled = pltpu.roll(plane, GRID_Y - cells_y, 1)
        turned_ref[k, :GRID_X, :] = rolled
        turned_ref[k, GRID_X:, :] = rolled[:extra]

    stride = round_up(pad_y, 16)
    side_ref[...] = jnp.zeros_like(side_ref)
    groups = pad_x // 8

    def gather_cell(cell, i, j):
        low_x, frac_x = split_cells(atoms_of(cell, 0), 0.0, cells_x)
        low_y, frac_y = split_cells(atoms_of(cell, 1), 0.0, cells_y)
        values, slopes = spline_weights(frac_x)
        wx_ref[...] = spline_table(low_x, values, pad_x)
        vx_ref[...] = spline_table(low_x, slopes, pad_x)
        for place, terms in enumerate(spline_weights(frac_y)):
            high, low = halves(spline_table(low_y, terms, stride))
            span = pl.ds(place * atom_total, atom_total)
            side_ref[:stride, span] = high
            side_ref[pl.ds(stride, stride), span] = low
            side_ref[pl.ds(2 * stride, stride), span] = high
        frac_z = atoms_of(cell, 5)
        deep, steep = depth_rows(table, atoms_of(cell, 4), frac_z, spline_weights(frac_z))
        source = mesh_ref if j % 2 == 0 else turned_ref
        rows = pl.ds(pl.multiple_of(i * cells_x, 8), pad_x)
        block = source[:, rows, pl.ds(j // 2 * window, window)].reshape(depth * pad_x, window)
        high = block.astype(jnp.bfloat16).astype(jnp.float32)
        low = block - high
        shifted = pltpu.roll(high, stride, 1)
        stack_ref[:, :window] = jnp.where(lane < stride, high, shifted).astype(jnp.bfloat16)
        stack_ref[:, window:] = jnp.where(
            lane < 2 * stride - window, shifted, pltpu.roll(low, 2 * stride - window, 1)
        ).astype(jnp.bfloat16)
        level_ref[...] = dot(stack_ref[...], side_ref[...])
        zero = jnp.zeros((8, atom_total), jnp.float32)
        first, second, third = (zero, zero, zero)
        for k in range(depth):
            flat = level_ref[pl.ds(k * pad_x, pad_x), :atom_total]
            tilt = level_ref[pl.ds(k * pad_x, pad_x), atom_total:]
            weight = wx_ref[...]
            part_x = jnp.sum((vx_ref[...] * flat).reshape(groups, 8, atom_total), axis=0)
            part_y = jnp.sum((weight * tilt).reshape(groups, 8, atom_total), axis=0)
            part_z = jnp.sum((weight * flat).reshape(groups, 8, atom_total), axis=0)
            first = first + deep[k : k + 1, :] * part_x
            second = second + deep[k : k + 1, :] * part_y
            third = third + steep[k : k + 1, :] * part_z
        for place, value in enumerate((first, second, third)):
            out_ref[cell, pl.ds(place, 1), :] = jnp.sum(value, axis=0, keepdims=True)

    @pl.loop(0, count_x)
    def _(i):
        for j in range(count_y):
            gather_cell(i * count_y + j, i, j)


def green_factors(index, period):
    signed = jnp.where(index <= period // 2, index, index - period).astype(jnp.float32) / (
        period * spacing
    )
    modulus = ((2.0 + jnp.cos(index.astype(jnp.float32) * (2.0 * jnp.pi / period))) / 3.0) ** 2
    square = signed * signed
    return jnp.stack([square, jnp.exp(-((jnp.pi / ewald_split) ** 2) * square) / modulus])


def one_cluster(own_rows, partner):
    offsets = (own_rows[:3, :, None] - partner[:3, None, :]) * spacing
    dist_square = jnp.sum(offsets * offsets, axis=0)
    soft_square = dist_square + soft_core
    soft_dist = jnp.sqrt(soft_square)
    scaled = ewald_split * soft_dist
    strength = (
        jax.scipy.special.erfc(scaled) / soft_dist
        + ewald_split * root_factor * jnp.exp(-scaled * scaled)
    ) / soft_square
    cutoff_taper = jnp.where(
        dist_square < cutoff * cutoff, (1.0 - dist_square / (cutoff * cutoff)) ** 2, 0.0
    )
    weight = partner[3][None, :] * strength * cutoff_taper
    return own_rows[3] * jnp.sum(weight[None] * offsets, axis=2)


def far_by_planes(gathered, own_charge, count_x, count_y, cells_x, cells_y):
    devices = count_x * count_y
    place = lax.axis_index("gx") * count_y + lax.axis_index("gy")
    depth = GRID_Z // devices
    atom_total = gathered.shape[2]
    pad_x = round_up(cells_x + 3, 8)
    pad_y = round_up(cells_y + 3, 8)
    window = 2 * cells_y
    turn_x = halves(jnp.asarray(hartley(GRID_X)))
    turn_y = halves(jnp.asarray(hartley(GRID_Y)))
    volume = GRID_X * GRID_Y * GRID_Z * spacing**3
    column = green_factors(jnp.arange(GRID_X, dtype=jnp.int32), GRID_X).T
    row = green_factors(jnp.arange(GRID_Y, dtype=jnp.int32), GRID_Y)
    own_k = place * depth + jnp.arange(depth, dtype=jnp.int32)
    deep = green_factors(own_k, GRID_Z)
    deep = (deep * jnp.array([[1.0], [1.0 / (math.pi * volume)]], jnp.float32)).T[:, None, :]
    taps = (own_k[:, None] * jnp.arange(4, dtype=jnp.int32)).astype(jnp.float32)
    taps = taps * (2.0 * math.pi / GRID_Z)
    cosine, sine = (jnp.cos(taps), jnp.sin(taps))
    table = jnp.concatenate(
        [own_k[:, None].astype(jnp.float32), cosine + sine, cosine - sine], axis=1
    )
    vmem = pl.BlockSpec(memory_space=pltpu.VMEM)
    rows = GRID_X + pad_x - cells_x
    partial = pl.pallas_call(
        functools.partial(mesh_kernel, (count_x, count_y), (cells_x, cells_y), (pad_x, pad_y)),
        in_specs=[vmem] * 9,
        out_specs=vmem,
        out_shape=jax.ShapeDtypeStruct((devices, 3, atom_total), jnp.float32),
        scratch_shapes=[
            pltpu.VMEM((pad_x, atom_total), jnp.float32),
            pltpu.VMEM((pad_x, atom_total), jnp.float32),
            pltpu.VMEM((2 * window, atom_total), jnp.bfloat16),
            pltpu.VMEM((depth * pad_x, atom_total), jnp.bfloat16),
            pltpu.VMEM((depth * pad_x, atom_total), jnp.bfloat16),
            pltpu.VMEM((depth, rows, GRID_Y), jnp.float32),
            pltpu.VMEM((depth, rows, GRID_Y), jnp.float32),
            pltpu.VMEM((depth * pad_x, 2 * atom_total), jnp.float32),
            pltpu.VMEM((depth * pad_x, 2 * window), jnp.bfloat16),
            pltpu.VMEM((2 * window, 2 * atom_total), jnp.bfloat16),
        ],
        name="mesh",
    )(gathered, *turn_x, *turn_y, column, row, deep, table)
    parts = lax.all_to_all(
        partial.reshape(devices, 3 * atom_total // 128, 128),
        ("gx", "gy"),
        split_axis=0,
        concat_axis=0,
        tiled=True,
    )
    total = jnp.sum(parts, axis=0).reshape(3, atom_total)
    return total * (-own_charge / spacing)


def convolved_by_lines(charge_mesh, count_x, count_y):
    turn_x = jnp.asarray(hartley(GRID_X))
    turn_y = jnp.asarray(hartley(GRID_Y))
    product = functools.partial(
        jnp.einsum, precision=lax.Precision.HIGHEST, preferred_element_type=jnp.float32
    )
    exchange = functools.partial(lax.all_to_all, tiled=True)
    lines = exchange(charge_mesh, "gx", split_axis=2, concat_axis=0)
    lines = product("xyk,xu->uyk", lines, turn_x)
    lines = exchange(lines, "gy", split_axis=0, concat_axis=1)
    lines = product("uyk,yv->uvk", lines, turn_y)
    wide, _, depth = lines.shape
    start_x = lax.axis_index("gy") * wide
    start_z = lax.axis_index("gx") * depth
    volume = GRID_X * GRID_Y * GRID_Z * spacing**3
    fx = green_factors(start_x + jnp.arange(wide, dtype=jnp.int32), GRID_X)
    fy = green_factors(jnp.arange(GRID_Y, dtype=jnp.int32), GRID_Y)
    fz = green_factors(start_z + jnp.arange(depth, dtype=jnp.int32), GRID_Z)
    square = fx[0][:, None, None] + fy[0][:, None] + fz[0]
    scale = fx[1][:, None, None] * fy[1][:, None] * fz[1] / (math.pi * volume)
    lines = lines * jnp.where(square > 0.0, scale / jnp.where(square > 0.0, square, 1.0), 0.0)
    lines = product("uvk,vy->uyk", lines, turn_y)
    lines = exchange(lines, "gy", split_axis=1, concat_axis=0)
    lines = product("uyk,ux->xyk", lines, turn_x)
    return exchange(lines, "gx", split_axis=0, concat_axis=2)


def far_by_lines(atoms, base, count_x, count_y, cells_x, cells_y, cells_z):
    atom_total = atoms.shape[1]
    cells = (cells_x, cells_y, cells_z)
    pad = (round_up(cells_x + 3, rows_group), round_up(cells_y + 3, 8))
    pad_x, pad_y = pad
    turn_z = jnp.asarray(hartley(GRID_Z))
    spread = pl.pallas_call(
        functools.partial(spread_kernel, cells, pad),
        out_shape=jax.ShapeDtypeStruct((pad_x, pad_y, GRID_Z), jnp.float32),
        scratch_shapes=[
            pltpu.VMEM((pad_x, atom_total), jnp.float32),
            pltpu.VMEM((pad_y, atom_total), jnp.float32),
            pltpu.VMEM((atom_total, 2 * GRID_Z), jnp.bfloat16),
            pltpu.VMEM((rows_group * pad_y, atom_total), jnp.bfloat16),
            pltpu.VMEM((rows_group * pad_y, atom_total), jnp.bfloat16),
        ],
        name="spread",
    )(atoms, base, turn_z)

    from_x = moved(spread[cells_x : cells_x + 3, :cells_y], 1, 0)
    from_y = moved(spread[:cells_x, cells_y : cells_y + 3], 0, 1)
    from_both = moved(spread[cells_x : cells_x + 3, cells_y : cells_y + 3], 1, 1)
    charge_mesh = (
        spread[:cells_x, :cells_y]
        .at[:3]
        .add(from_x)
        .at[:, :3]
        .add(from_y)
        .at[:3, :3]
        .add(from_both)
    )
    potential = convolved_by_lines(charge_mesh, count_x, count_y)
    upper_x = moved(potential[:3], -1, 0)
    upper_y = moved(potential[:, :3], 0, -1)
    upper_both = moved(potential[:3, :3], -1, -1)
    wider = jnp.concatenate(
        [
            jnp.concatenate([potential, upper_x], axis=0),
            jnp.concatenate([upper_y, upper_both], axis=0),
        ],
        axis=1,
    )
    wider = jnp.pad(wider, ((0, pad_x - cells_x - 3), (0, pad_y - cells_y - 3), (0, 0)))
    return pl.pallas_call(
        functools.partial(gather_kernel, cells, pad),
        out_shape=jax.ShapeDtypeStruct((3, atom_total), jnp.float32),
        scratch_shapes=[
            pltpu.VMEM((pad_x, atom_total), jnp.float32),
            pltpu.VMEM((pad_x, atom_total), jnp.float32),
            pltpu.VMEM((pad_y, atom_total), jnp.float32),
            pltpu.VMEM((pad_y, atom_total), jnp.float32),
            pltpu.VMEM((2 * GRID_Z, 2 * atom_total), jnp.bfloat16),
            pltpu.VMEM((rows_group * pad_y, 2 * atom_total), jnp.float32),
        ],
        name="gather",
    )(atoms, base, turn_z, wider)


def local(positions, charges, pair_lists, slab_dest, atom_counts):
    count_x = lax.axis_size("gx")
    count_y = lax.axis_size("gy")
    devices = count_x * count_y
    atom_total = positions.shape[3]
    clusters = pair_lists.shape[2]
    cluster_size = atom_total // clusters
    blocks = slab_dest.shape[2]
    block_size = atom_total // blocks
    cells_x = GRID_X // count_x
    cells_y = GRID_Y // count_y
    cells_z = GRID_Z // count_y
    living = jnp.arange(atom_total, dtype=jnp.int32) < atom_counts[0, 0]
    charge = jnp.where(living, charges[0, 0], 0.0)
    packed = jnp.concatenate([positions, charge[None, None, None, :]], axis=0)
    atoms = packed.reshape(4, atom_total)

    base = jnp.broadcast_to(
        (slab_dest[0, 0] * cells_z)[:, None], (blocks, block_size)
    ).reshape(1, atom_total)
    height, fraction = split_cells(
        atoms[2], base[0].astype(jnp.float32), cells_z
    )
    height = (base[0] + height).astype(jnp.float32)
    sent = jnp.stack([*atoms, height, fraction, fraction, fraction])
    gathered = lax.all_gather(sent, ("gx", "gy"), axis=0, tiled=False)
    by_planes = GRID_Z % devices == 0 and cells_y == 64 and cells_x % 8 == 0
    if by_planes:
        far_part = far_by_planes(gathered, charge, count_x, count_y, cells_x, cells_y)
    else:
        far_part = far_by_lines(atoms, base, count_x, count_y, cells_x, cells_y, cells_z)

    chosen = pair_lists[0, 0]
    beside = chosen // clusters
    step_x, step_y = (beside // 3 - 1, beside % 3 - 1)
    at_x = (lax.axis_index("gx") + step_x + count_x) % count_x
    at_y = (lax.axis_index("gy") + step_y + count_y) % count_y
    number = (at_x * count_y + at_y) * clusters + chosen % clusters
    pick = (number[:, :, None] == jnp.arange(devices * clusters, dtype=jnp.int32)).astype(
        jnp.float32
    )
    pool = gathered[:, :4].reshape(devices, 4, clusters, cluster_size)
    pool = jnp.transpose(pool, (1, 0, 2, 3)).reshape(4, devices * clusters, cluster_size)
    partners = jnp.einsum(
        "cln,fnk->cflk",
        pick,
        pool,
        precision=lax.Precision.HIGHEST,
        preferred_element_type=jnp.float32,
    )
    shift_x = (step_x * cells_x).astype(jnp.float32)
    shift_y = (step_y * cells_y).astype(jnp.float32)
    flat = jnp.zeros_like(shift_x)
    shift = jnp.stack([shift_x, shift_y, flat, flat], axis=1)
    partners = (partners + shift[:, :, :, None]).reshape(clusters, 4, -1)
    own = packed.reshape(4, clusters, cluster_size)
    pair_part = jnp.stack(
        [one_cluster(own[:, c], partners[c]) for c in range(clusters)], axis=1
    )
    short_forces = pair_part.reshape(3, 1, 1, atom_total)
    return (short_forces, far_part.reshape(3, 1, 1, atom_total))


def solution(mesh):
    return jax.shard_map(
        local,
        mesh=mesh,
        in_specs=(
            P(None, ("rep", "gx"), "gy", None),
            P(("rep", "gx"), "gy", None),
            P(("rep", "gx"), "gy", None, None),
            P(("rep", "gx"), "gy", None),
            P(("rep", "gx"), "gy"),
        ),
        out_specs=(P(None, ("rep", "gx"), "gy", None), P(None, ("rep", "gx"), "gy", None)),
        check_vma=False,
    )
```

```python
import functools
import math

import jax
import jax.numpy as jnp
import numpy as np
from jax import lax
from jax.experimental import pallas as pl
from jax.experimental.pallas import tpu as pltpu
from jax.sharding import PartitionSpec as P

GRID_X = 256
GRID_Y = 256
GRID_Z = 128


spacing = 0.16
ewald_split = 3.47
cutoff = 0.9
soft_core = 0.09
root_factor = 1.1283791670955126
rows_group = 8


def moved(value, step_x, step_y):
    count_x = lax.axis_size("gx")
    count_y = lax.axis_size("gy")
    pairs = [
        (i * count_y + j, (i + step_x) % count_x * count_y + (j + step_y) % count_y)
        for i in range(count_x)
        for j in range(count_y)
    ]
    return lax.ppermute(value, ("gx", "gy"), pairs)


def round_up(value, multiple):
    return -(-value // multiple) * multiple


def hartley(period):
    turns = np.outer(np.arange(period), np.arange(period)) % period
    phases = turns * (2.0 * np.pi / period)
    return (np.cos(phases) + np.sin(phases)).astype(np.float32)


def halves(value):
    high = value.astype(jnp.bfloat16)
    low = (value - high.astype(jnp.float32)).astype(jnp.bfloat16)
    return (high, low)


def dot(left_side, right_side):
    return jnp.dot(left_side, right_side, preferred_element_type=jnp.float32)


def spline_weights(fraction):
    remain = 1.0 - fraction
    square = fraction * fraction
    cube_part = square * fraction
    values = [
        remain * remain * remain / 6.0,
        (3.0 * cube_part - 6.0 * square + 4.0) / 6.0,
        (-3.0 * cube_part + 3.0 * square + 3.0 * fraction + 1.0) / 6.0,
        cube_part / 6.0,
    ]
    slopes = [
        -0.5 * remain * remain,
        0.5 * (3.0 * square - 4.0 * fraction),
        0.5 * (-3.0 * square + 2.0 * fraction + 1.0),
        0.5 * square,
    ]
    return (values, slopes)


def split_cells(coordinate, offset, cell_count):
    inside = coordinate - offset
    lowest = jnp.clip(jnp.floor(inside).astype(jnp.int32), 0, cell_count - 1)
    return (lowest, inside - lowest.astype(inside.dtype))


def spline_table(lowest, values, table_size, period=None):
    points = lax.broadcasted_iota(jnp.int32, (table_size, lowest.shape[1]), 0)
    lookup = jnp.zeros(points.shape, jnp.float32)
    for spline_term in range(4):
        at = lowest + spline_term
        if period is not None:
            at = jnp.where(at >= period, at - period, at)
        lookup = jnp.where(points == at, values[spline_term], lookup)
    return lookup


def spread_kernel(cells, pad, atoms_ref, base_ref, turn_ref, out_ref, wx_ref, wy_ref, wz_ref, hi_ref, lo_ref):
    cells_x, cells_y, cells_z = cells
    pad_x, pad_y = pad
    atom_total = atoms_ref.shape[1]
    low_x, frac_x = split_cells(atoms_ref[0:1, :], 0.0, cells_x)
    low_y, frac_y = split_cells(atoms_ref[1:2, :], 0.0, cells_y)
    base = base_ref[...]
    low_z, frac_z = split_cells(atoms_ref[2:3, :], base.astype(jnp.float32), cells_z)
    wx_ref[...] = spline_table(low_x, spline_weights(frac_x)[0], pad_x) * atoms_ref[3:4, :]
    wy_ref[...] = spline_table(low_y, spline_weights(frac_y)[0], pad_y)
    turn = turn_ref[...]
    size_z = turn.shape[0]
    table_z = spline_table(base + low_z, spline_weights(frac_z)[0], size_z, size_z)
    waves = jnp.dot(
        turn, table_z, precision=lax.Precision.HIGHEST, preferred_element_type=jnp.float32
    ).T
    high, low = halves(waves)
    wz_ref[:, :size_z] = high
    wz_ref[:, size_z:] = low

    @pl.loop(0, pad_x // rows_group)
    def _(chunk):
        for inner in range(rows_group):
            row = wx_ref[pl.ds(chunk * rows_group + inner, 1), :]
            high, low = halves(row * wy_ref[...])
            hi_ref[pl.ds(inner * pad_y, pad_y), :] = high
            lo_ref[pl.ds(inner * pad_y, pad_y), :] = low
        both = dot(hi_ref[...], wz_ref[...])
        rest = dot(lo_ref[...], wz_ref[:, :size_z])
        total = both[:, :size_z] + both[:, size_z:] + rest
        out_ref[pl.ds(chunk * rows_group, rows_group)] = total.reshape(rows_group, pad_y, size_z)


def gather_kernel(cells, pad, atoms_ref, base_ref, turn_ref, mesh_ref, out_ref, wx_ref, vx_ref, wy_ref, vy_ref, wz_ref, level_ref):
    cells_x, cells_y, cells_z = cells
    pad_x, pad_y = pad
    atom_total = atoms_ref.shape[1]
    low_x, frac_x = split_cells(atoms_ref[0:1, :], 0.0, cells_x)
    low_y, frac_y = split_cells(atoms_ref[1:2, :], 0.0, cells_y)
    base = base_ref[...]
    low_z, frac_z = split_cells(atoms_ref[2:3, :], base.astype(jnp.float32), cells_z)
    values, slopes = spline_weights(frac_x)
    wx_ref[...] = spline_table(low_x, values, pad_x)
    vx_ref[...] = spline_table(low_x, slopes, pad_x)
    values, slopes = spline_weights(frac_y)
    wy_ref[...] = spline_table(low_y, values, pad_y)
    vy_ref[...] = spline_table(low_y, slopes, pad_y)
    values, slopes = spline_weights(frac_z)
    turn = turn_ref[...]
    size_z = turn.shape[0]
    for place, terms in enumerate((values, slopes)):
        table_z = spline_table(base + low_z, terms, size_z, size_z)
        waves = jnp.dot(
            turn, table_z, precision=lax.Precision.HIGHEST, preferred_element_type=jnp.float32
        )
        high, low = halves(waves)
        wz_ref[:size_z, pl.ds(place * atom_total, atom_total)] = high
        wz_ref[size_z:, pl.ds(place * atom_total, atom_total)] = low
    groups = pad_y // 8

    def one_chunk(chunk, sums):
        rows = mesh_ref[pl.ds(chunk * rows_group, rows_group)].reshape(rows_group * pad_y, size_z)
        high, low = halves(rows)
        level_ref[...] = dot(jnp.concatenate([high, high], axis=1), wz_ref[...]) + dot(
            low, wz_ref[:size_z, :]
        )
        first, second, third = sums
        for inner in range(rows_group):
            flat = level_ref[pl.ds(inner * pad_y, pad_y), :atom_total]
            tilt = level_ref[pl.ds(inner * pad_y, pad_y), atom_total:]
            across = wy_ref[...]
            part_x = jnp.sum((across * flat).reshape(groups, 8, atom_total), axis=0)
            part_y = jnp.sum((vy_ref[...] * flat).reshape(groups, 8, atom_total), axis=0)
            part_z = jnp.sum((across * tilt).reshape(groups, 8, atom_total), axis=0)
            weight = wx_ref[pl.ds(chunk * rows_group + inner, 1), :]
            slope = vx_ref[pl.ds(chunk * rows_group + inner, 1), :]
            first = first + slope * part_x
            second = second + weight * part_y
            third = third + weight * part_z
        return (first, second, third)

    zero = jnp.zeros((8, atom_total), jnp.float32)
    sums = lax.fori_loop(0, pad_x // rows_group, one_chunk, (zero, zero, zero))
    factor = -atoms_ref[3:4, :] / spacing
    for place in range(3):
        out_ref[pl.ds(place, 1), :] = factor * jnp.sum(sums[place], axis=0, keepdims=True)


def share_kernel(sizes, atoms_ref, out_ref, send_sem, recv_sem):
    count_x, count_y = sizes
    place_x, place_y = (lax.axis_index("gx"), lax.axis_index("gy"))
    me = place_x * count_y + place_y
    peers = []
    for order in range(1, count_x * count_y):
        peer_x = lax.rem(place_x + order // count_y, count_x)
        peer_y = lax.rem(place_y + order % count_y, count_y)
        peers.append({"gx": peer_x, "gy": peer_y})
    barrier = pltpu.get_barrier_semaphore()
    for peer in peers:
        pl.semaphore_signal(
            barrier, inc=1, device_id=peer, device_id_type=pl.DeviceIdType.MESH
        )
    pl.semaphore_wait(barrier, len(peers))
    copies = [
        pltpu.make_async_remote_copy(
            src_ref=atoms_ref,
            dst_ref=out_ref.at[me],
            send_sem=send_sem.at[order],
            recv_sem=recv_sem.at[order],
            device_id=peer,
            device_id_type=pl.DeviceIdType.MESH,
        )
        for order, peer in enumerate(peers)
    ]
    for copy in copies:
        copy.start()
    out_ref[me] = atoms_ref[...]
    for copy in copies:
        copy.wait()


def shared(atoms, count_x, count_y):
    devices = count_x * count_y
    vmem = pl.BlockSpec(memory_space=pltpu.VMEM)
    flags = pltpu.SemaphoreType.DMA((devices - 1,))
    return pl.pallas_call(
        functools.partial(share_kernel, (count_x, count_y)),
        in_specs=[vmem],
        out_specs=vmem,
        out_shape=jax.ShapeDtypeStruct((devices, *atoms.shape), jnp.float32),
        scratch_shapes=[flags, flags],
        compiler_params=pltpu.CompilerParams(collective_id=0, has_side_effects=True),
        name="share",
    )(atoms)


def depth_rows(table, height, fraction, terms):
    turns = (height * table[:, 0:1]).astype(jnp.int32) % GRID_Z
    phases = turns.astype(jnp.float32) * (2.0 * math.pi / GRID_Z)
    cosine, sine = (jnp.cos(phases), jnp.sin(phases))
    results = []
    for weights in terms:
        even = sum(table[:, 1 + t : 2 + t] * weights[t] for t in range(4))
        odd = sum(table[:, 5 + t : 6 + t] * weights[t] for t in range(4))
        results.append(cosine * even + sine * odd)
    return results


def mesh_kernel(sizes, cells, pad, atoms_ref, xh_ref, xl_ref, yh_ref, yl_ref, column_ref, row_ref, table_ref, out_ref, mesh_ref, turned_ref, *scratch):
    count_x, count_y = sizes
    cells_x, cells_y = cells
    pad_x, pad_y = pad
    atom_total = atoms_ref.shape[2]
    depth = table_ref.shape[0]
    window = 2 * cells_y
    windows = GRID_Y // window
    lane = lax.broadcasted_iota(jnp.int32, (depth * pad_x, window), 1)
    mesh_ref[...] = jnp.zeros_like(mesh_ref)
    table = table_ref[...]
    per_side = len(scratch) // 2
    banks = (scratch[:per_side], scratch[per_side:])
    for _, _, wy_ref, _, _, _, _, side_ref in banks:
        wy_ref[...] = jnp.zeros_like(wy_ref)
        side_ref[...] = jnp.zeros_like(side_ref)

    def atoms_of(cell, row):
        return atoms_ref[cell, row : row + 1, :]

    def spread_cell(cell, i, j):
        wx_ref, vx_ref, wy_ref, hi_ref, lo_ref, level_ref, stack_ref, side_ref = banks[j % 2]
        low_x, frac_x = split_cells(atoms_of(cell, 0), 0.0, cells_x)
        low_y, frac_y = split_cells(atoms_of(cell, 1), 0.0, cells_y)
        wx_ref[...] = spline_table(low_x, spline_weights(frac_x)[0], pad_x)
        high, low = halves(spline_table(low_y, spline_weights(frac_y)[0], pad_y))
        wy_ref[:pad_y, :] = high
        wy_ref[pl.ds(window, pad_y), :] = low
        height = jnp.floor(atoms_of(cell, 2))
        frac_z = atoms_of(cell, 2) - height
        (deep,) = depth_rows(table, height, frac_z, [spline_weights(frac_z)[0]])
        deep = deep * atoms_of(cell, 3)
        for k in range(depth):
            high, low = halves(deep[k : k + 1, :] * wx_ref[...])
            hi_ref[pl.ds(k * pad_x, pad_x), :] = high
            lo_ref[pl.ds(k * pad_x, pad_x), :] = low
        numbers = (((1,), (1,)), ((), ()))
        both = lax.dot_general(
            hi_ref[...], wy_ref[...], numbers, preferred_element_type=jnp.float32
        )
        rest = lax.dot_general(
            lo_ref[...], wy_ref[:window, :], numbers, preferred_element_type=jnp.float32
        )
        total = both[:, :window] + both[:, window:] + rest
        rows = pl.ds(pl.multiple_of(i * cells_x, 8), pad_x)
        m = j // 2
        if j % 2 == 0:
            mesh_ref[:, rows, pl.ds(m * window, window)] += total.reshape(depth, pad_x, window)
        else:
            total = pltpu.roll(total, cells_y, 1)
            kept = jnp.where(lane >= cells_y, total, 0.0)
            carried = jnp.where(lane < cells_y, total, 0.0)
            after = (m + 1) % windows
            mesh_ref[:, rows, pl.ds(m * window, window)] += kept.reshape(depth, pad_x, window)
            mesh_ref[:, rows, pl.ds(after * window, window)] += carried.reshape(
                depth, pad_x, window
            )

    @pl.loop(0, count_x)
    def _(i):
        for j in range(count_y):
            spread_cell(i * count_y + j, i, j)

    def across(value):
        high, low = halves(value)
        return dot(xh_ref[...], high) + dot(xl_ref[...], high) + dot(xh_ref[...], low)

    def along(value):
        high, low = halves(value)
        return dot(high, yh_ref[...]) + dot(high, yl_ref[...]) + dot(low, yh_ref[...])

    extra = mesh_ref.shape[1] - GRID_X

    @pl.loop(0, depth)
    def _(k):
        mesh_ref[k, :extra, :] += mesh_ref[k, GRID_X:, :]
        waves = along(across(mesh_ref[k, :GRID_X, :]))
        square = column_ref[:, 0:1] + row_ref[0:1, :] + table_ref[pl.ds(k, 1), 9:10]
        scale = column_ref[:, 1:2] * row_ref[1:2, :] * table_ref[pl.ds(k, 1), 10:11]
        green = jnp.where(square > 0.0, scale / jnp.where(square > 0.0, square, 1.0), 0.0)
        plane = across(along(waves * green))
        mesh_ref[k, :GRID_X, :] = plane
        mesh_ref[k, GRID_X:, :] = plane[:extra]
        rolled = pltpu.roll(plane, GRID_Y - cells_y, 1)
        turned_ref[k, :GRID_X, :] = rolled
        turned_ref[k, GRID_X:, :] = rolled[:extra]

    stride = round_up(pad_y, 16)
    groups = pad_x // 8

    def gather_cell(cell, i, j):
        wx_ref, vx_ref, wy_ref, hi_ref, lo_ref, level_ref, stack_ref, side_ref = banks[j % 2]
        low_x, frac_x = split_cells(atoms_of(cell, 0), 0.0, cells_x)
        low_y, frac_y = split_cells(atoms_of(cell, 1), 0.0, cells_y)
        values, slopes = spline_weights(frac_x)
        wx_ref[...] = spline_table(low_x, values, pad_x)
        vx_ref[...] = spline_table(low_x, slopes, pad_x)
        for place, terms in enumerate(spline_weights(frac_y)):
            high, low = halves(spline_table(low_y, terms, stride))
            span = pl.ds(place * atom_total, atom_total)
            side_ref[:stride, span] = high
            side_ref[pl.ds(stride, stride), span] = low
            side_ref[pl.ds(2 * stride, stride), span] = high
        height = jnp.floor(atoms_of(cell, 2))
        frac_z = atoms_of(cell, 2) - height
        deep, steep = depth_rows(table, height, frac_z, spline_weights(frac_z))
        source = mesh_ref if j % 2 == 0 else turned_ref
        rows = pl.ds(pl.multiple_of(i * cells_x, 8), pad_x)
        block = source[:, rows, pl.ds(j // 2 * window, window)].reshape(depth * pad_x, window)
        high = block.astype(jnp.bfloat16).astype(jnp.float32)
        low = block - high
        shifted = pltpu.roll(high, stride, 1)
        stack_ref[:, :window] = jnp.where(lane < stride, high, shifted).astype(jnp.bfloat16)
        stack_ref[:, window:] = jnp.where(
            lane < 2 * stride - window, shifted, pltpu.roll(low, 2 * stride - window, 1)
        ).astype(jnp.bfloat16)
        level_ref[...] = dot(stack_ref[...], side_ref[...])
        zero = jnp.zeros((8, atom_total), jnp.float32)
        first, second, third = (zero, zero, zero)
        for k in range(depth):
            flat = level_ref[pl.ds(k * pad_x, pad_x), :atom_total]
            tilt = level_ref[pl.ds(k * pad_x, pad_x), atom_total:]
            weight = wx_ref[...]
            part_x = jnp.sum((vx_ref[...] * flat).reshape(groups, 8, atom_total), axis=0)
            part_y = jnp.sum((weight * tilt).reshape(groups, 8, atom_total), axis=0)
            part_z = jnp.sum((weight * flat).reshape(groups, 8, atom_total), axis=0)
            first = first + deep[k : k + 1, :] * part_x
            second = second + deep[k : k + 1, :] * part_y
            third = third + steep[k : k + 1, :] * part_z
        for place, value in enumerate((first, second, third)):
            out_ref[cell, pl.ds(place, 1), :] = jnp.sum(value, axis=0, keepdims=True)
        out_ref[cell, 3:4, :] = jnp.zeros((1, atom_total), jnp.float32)

    @pl.loop(0, count_x)
    def _(i):
        for j in range(count_y):
            gather_cell(i * count_y + j, i, j)


def green_table(period):
    index = np.arange(period)
    signed = np.where(index <= period // 2, index, index - period) / (period * spacing)
    modulus = ((2.0 + np.cos(index * (2.0 * np.pi / period))) / 3.0) ** 2
    square = signed * signed
    return np.stack([square, np.exp(-((np.pi / ewald_split) ** 2) * square) / modulus]).astype(
        np.float32
    )


def green_factors(index, period):
    signed = jnp.where(index <= period // 2, index, index - period).astype(jnp.float32) / (
        period * spacing
    )
    modulus = ((2.0 + jnp.cos(index.astype(jnp.float32) * (2.0 * jnp.pi / period))) / 3.0) ** 2
    square = signed * signed
    return jnp.stack([square, jnp.exp(-((jnp.pi / ewald_split) ** 2) * square) / modulus])


def one_cluster(own_rows, partner):
    offsets = (own_rows[:3, :, None] - partner[:3, None, :]) * spacing
    dist_square = jnp.sum(offsets * offsets, axis=0)
    soft_square = dist_square + soft_core
    soft_dist = jnp.sqrt(soft_square)
    scaled = ewald_split * soft_dist
    strength = (
        jax.scipy.special.erfc(scaled) / soft_dist
        + ewald_split * root_factor * jnp.exp(-scaled * scaled)
    ) / soft_square
    cutoff_taper = jnp.where(
        dist_square < cutoff * cutoff, (1.0 - dist_square / (cutoff * cutoff)) ** 2, 0.0
    )
    weight = partner[3][None, :] * strength * cutoff_taper
    return own_rows[3] * jnp.sum(weight[None] * offsets, axis=2)


def far_by_planes(gathered, own_charge, count_x, count_y, cells_x, cells_y):
    devices = count_x * count_y
    place = lax.axis_index("gx") * count_y + lax.axis_index("gy")
    depth = GRID_Z // devices
    atom_total = gathered.shape[2]
    pad_x = round_up(cells_x + 3, 8)
    pad_y = round_up(cells_y + 3, 8)
    window = 2 * cells_y
    turn_x = halves(jnp.asarray(hartley(GRID_X)))
    turn_y = halves(jnp.asarray(hartley(GRID_Y)))
    volume = GRID_X * GRID_Y * GRID_Z * spacing**3
    column = jnp.asarray(green_table(GRID_X).T)
    row = jnp.asarray(green_table(GRID_Y))
    every_k = np.arange(GRID_Z)
    taps = np.outer(every_k, np.arange(4)) * (2.0 * np.pi / GRID_Z)
    square, scale = green_table(GRID_Z)
    table = np.concatenate(
        [
            every_k[:, None],
            np.cos(taps) + np.sin(taps),
            np.cos(taps) - np.sin(taps),
            square[:, None],
            scale[:, None] / (np.pi * volume),
        ],
        axis=1,
    ).astype(np.float32)
    table = lax.dynamic_slice_in_dim(jnp.asarray(table), place * depth, depth, axis=0)
    vmem = pl.BlockSpec(memory_space=pltpu.VMEM)
    rows = GRID_X + pad_x - cells_x
    bank = [
        pltpu.VMEM((pad_x, atom_total), jnp.float32),
        pltpu.VMEM((pad_x, atom_total), jnp.float32),
        pltpu.VMEM((2 * window, atom_total), jnp.bfloat16),
        pltpu.VMEM((depth * pad_x, atom_total), jnp.bfloat16),
        pltpu.VMEM((depth * pad_x, atom_total), jnp.bfloat16),
        pltpu.VMEM((depth * pad_x, 2 * atom_total), jnp.float32),
        pltpu.VMEM((depth * pad_x, 2 * window), jnp.bfloat16),
        pltpu.VMEM((2 * window, 2 * atom_total), jnp.bfloat16),
    ]
    partial = pl.pallas_call(
        functools.partial(mesh_kernel, (count_x, count_y), (cells_x, cells_y), (pad_x, pad_y)),
        in_specs=[vmem] * 8,
        out_specs=vmem,
        out_shape=jax.ShapeDtypeStruct((devices, 4, atom_total), jnp.float32),
        scratch_shapes=[pltpu.VMEM((depth, rows, GRID_Y), jnp.float32)] * 2 + 2 * bank,
        name="mesh",
    )(gathered, *turn_x, *turn_y, column, row, table)
    parts = lax.all_to_all(partial, ("gx", "gy"), split_axis=0, concat_axis=0, tiled=True)
    total = jnp.sum(parts, axis=0)[:3]
    return total * (-own_charge / spacing)


def convolved_by_lines(charge_mesh, count_x, count_y):
    turn_x = jnp.asarray(hartley(GRID_X))
    turn_y = jnp.asarray(hartley(GRID_Y))
    product = functools.partial(
        jnp.einsum, precision=lax.Precision.HIGHEST, preferred_element_type=jnp.float32
    )
    exchange = functools.partial(lax.all_to_all, tiled=True)
    lines = exchange(charge_mesh, "gx", split_axis=2, concat_axis=0)
    lines = product("xyk,xu->uyk", lines, turn_x)
    lines = exchange(lines, "gy", split_axis=0, concat_axis=1)
    lines = product("uyk,yv->uvk", lines, turn_y)
    wide, _, depth = lines.shape
    start_x = lax.axis_index("gy") * wide
    start_z = lax.axis_index("gx") * depth
    volume = GRID_X * GRID_Y * GRID_Z * spacing**3
    fx = green_factors(start_x + jnp.arange(wide, dtype=jnp.int32), GRID_X)
    fy = green_factors(jnp.arange(GRID_Y, dtype=jnp.int32), GRID_Y)
    fz = green_factors(start_z + jnp.arange(depth, dtype=jnp.int32), GRID_Z)
    square = fx[0][:, None, None] + fy[0][:, None] + fz[0]
    scale = fx[1][:, None, None] * fy[1][:, None] * fz[1] / (math.pi * volume)
    lines = lines * jnp.where(square > 0.0, scale / jnp.where(square > 0.0, square, 1.0), 0.0)
    lines = product("uvk,vy->uyk", lines, turn_y)
    lines = exchange(lines, "gy", split_axis=1, concat_axis=0)
    lines = product("uyk,ux->xyk", lines, turn_x)
    return exchange(lines, "gx", split_axis=0, concat_axis=2)


def far_by_lines(atoms, base, count_x, count_y, cells_x, cells_y, cells_z):
    atom_total = atoms.shape[1]
    cells = (cells_x, cells_y, cells_z)
    pad = (round_up(cells_x + 3, rows_group), round_up(cells_y + 3, 8))
    pad_x, pad_y = pad
    turn_z = jnp.asarray(hartley(GRID_Z))
    spread = pl.pallas_call(
        functools.partial(spread_kernel, cells, pad),
        out_shape=jax.ShapeDtypeStruct((pad_x, pad_y, GRID_Z), jnp.float32),
        scratch_shapes=[
            pltpu.VMEM((pad_x, atom_total), jnp.float32),
            pltpu.VMEM((pad_y, atom_total), jnp.float32),
            pltpu.VMEM((atom_total, 2 * GRID_Z), jnp.bfloat16),
            pltpu.VMEM((rows_group * pad_y, atom_total), jnp.bfloat16),
            pltpu.VMEM((rows_group * pad_y, atom_total), jnp.bfloat16),
        ],
        name="spread",
    )(atoms, base, turn_z)

    from_x = moved(spread[cells_x : cells_x + 3, :cells_y], 1, 0)
    from_y = moved(spread[:cells_x, cells_y : cells_y + 3], 0, 1)
    from_both = moved(spread[cells_x : cells_x + 3, cells_y : cells_y + 3], 1, 1)
    charge_mesh = (
        spread[:cells_x, :cells_y]
        .at[:3]
        .add(from_x)
        .at[:, :3]
        .add(from_y)
        .at[:3, :3]
        .add(from_both)
    )
    potential = convolved_by_lines(charge_mesh, count_x, count_y)
    upper_x = moved(potential[:3], -1, 0)
    upper_y = moved(potential[:, :3], 0, -1)
    upper_both = moved(potential[:3, :3], -1, -1)
    wider = jnp.concatenate(
        [
            jnp.concatenate([potential, upper_x], axis=0),
            jnp.concatenate([upper_y, upper_both], axis=0),
        ],
        axis=1,
    )
    wider = jnp.pad(wider, ((0, pad_x - cells_x - 3), (0, pad_y - cells_y - 3), (0, 0)))
    return pl.pallas_call(
        functools.partial(gather_kernel, cells, pad),
        out_shape=jax.ShapeDtypeStruct((3, atom_total), jnp.float32),
        scratch_shapes=[
            pltpu.VMEM((pad_x, atom_total), jnp.float32),
            pltpu.VMEM((pad_x, atom_total), jnp.float32),
            pltpu.VMEM((pad_y, atom_total), jnp.float32),
            pltpu.VMEM((pad_y, atom_total), jnp.float32),
            pltpu.VMEM((2 * GRID_Z, 2 * atom_total), jnp.bfloat16),
            pltpu.VMEM((rows_group * pad_y, 2 * atom_total), jnp.float32),
        ],
        name="gather",
    )(atoms, base, turn_z, wider)


def local(positions, charges, pair_lists, slab_dest, atom_counts):
    count_x = lax.axis_size("gx")
    count_y = lax.axis_size("gy")
    devices = count_x * count_y
    atom_total = positions.shape[3]
    clusters = pair_lists.shape[2]
    cluster_size = atom_total // clusters
    blocks = slab_dest.shape[2]
    block_size = atom_total // blocks
    cells_x = GRID_X // count_x
    cells_y = GRID_Y // count_y
    cells_z = GRID_Z // count_y
    living = jnp.arange(atom_total, dtype=jnp.int32) < atom_counts[0, 0]
    charge = jnp.where(living, charges[0, 0], 0.0)
    packed = jnp.concatenate([positions, charge[None, None, None, :]], axis=0)
    atoms = packed.reshape(4, atom_total)

    base = jnp.broadcast_to(
        (slab_dest[0, 0] * cells_z)[:, None], (blocks, block_size)
    ).reshape(1, atom_total)
    by_planes = GRID_Z % devices == 0 and cells_y == 64 and cells_x % 8 == 0
    if by_planes:
        gathered = shared(atoms, count_x, count_y)
    else:
        gathered = lax.all_gather(atoms, ("gx", "gy"), axis=0, tiled=False)
    if by_planes:
        far_part = far_by_planes(gathered, charge, count_x, count_y, cells_x, cells_y)
    else:
        far_part = far_by_lines(atoms, base, count_x, count_y, cells_x, cells_y, cells_z)

    chosen = pair_lists[0, 0]
    beside = chosen // clusters
    step_x, step_y = (beside // 3 - 1, beside % 3 - 1)
    at_x = (lax.axis_index("gx") + step_x + count_x) % count_x
    at_y = (lax.axis_index("gy") + step_y + count_y) % count_y
    number = (at_x * count_y + at_y) * clusters + chosen % clusters
    pick = (number[:, :, None] == jnp.arange(devices * clusters, dtype=jnp.int32)).astype(
        jnp.float32
    )
    pool = gathered[:, :4].reshape(devices, 4, clusters, cluster_size)
    pool = jnp.transpose(pool, (1, 0, 2, 3)).reshape(4, devices * clusters, cluster_size)
    partners = jnp.einsum(
        "cln,fnk->cflk",
        pick,
        pool,
        precision=lax.Precision.HIGHEST,
        preferred_element_type=jnp.float32,
    )
    shift_x = (step_x * cells_x).astype(jnp.float32)
    shift_y = (step_y * cells_y).astype(jnp.float32)
    flat = jnp.zeros_like(shift_x)
    shift = jnp.stack([shift_x, shift_y, flat, flat], axis=1)
    partners = (partners + shift[:, :, :, None]).reshape(clusters, 4, -1)
    own = packed.reshape(4, clusters, cluster_size)
    pair_part = jnp.stack(
        [one_cluster(own[:, c], partners[c]) for c in range(clusters)], axis=1
    )
    short_forces = pair_part.reshape(3, 1, 1, atom_total)
    return (short_forces, far_part.reshape(3, 1, 1, atom_total))


def solution(mesh):
    return jax.shard_map(
        local,
        mesh=mesh,
        in_specs=(
            P(None, ("rep", "gx"), "gy", None),
            P(("rep", "gx"), "gy", None),
            P(("rep", "gx"), "gy", None, None),
            P(("rep", "gx"), "gy", None),
            P(("rep", "gx"), "gy"),
        ),
        out_specs=(P(None, ("rep", "gx"), "gy", None), P(None, ("rep", "gx"), "gy", None)),
        check_vma=False,
    )
```

```python
import functools
import math

import jax
import jax.numpy as jnp
import numpy as np
from jax import lax
from jax.experimental import pallas as pl
from jax.experimental.pallas import tpu as pltpu
from jax.sharding import PartitionSpec as P

GRID_X = 256
GRID_Y = 256
GRID_Z = 128


spacing = 0.16
ewald_split = 3.47
cutoff = 0.9
soft_core = 0.09
root_factor = 1.1283791670955126
rows_group = 8


def moved(value, step_x, step_y):
    count_x = lax.axis_size("gx")
    count_y = lax.axis_size("gy")
    pairs = [
        (i * count_y + j, (i + step_x) % count_x * count_y + (j + step_y) % count_y)
        for i in range(count_x)
        for j in range(count_y)
    ]
    return lax.ppermute(value, ("gx", "gy"), pairs)


def round_up(value, multiple):
    return -(-value // multiple) * multiple


def hartley(period):
    turns = np.outer(np.arange(period), np.arange(period)) % period
    phases = turns * (2.0 * np.pi / period)
    return (np.cos(phases) + np.sin(phases)).astype(np.float32)


def halves(value):
    high = value.astype(jnp.bfloat16)
    low = (value - high.astype(jnp.float32)).astype(jnp.bfloat16)
    return (high, low)


def dot(left_side, right_side):
    return jnp.dot(left_side, right_side, preferred_element_type=jnp.float32)


def spline_weights(fraction):
    remain = 1.0 - fraction
    square = fraction * fraction
    cube_part = square * fraction
    values = [
        remain * remain * remain / 6.0,
        (3.0 * cube_part - 6.0 * square + 4.0) / 6.0,
        (-3.0 * cube_part + 3.0 * square + 3.0 * fraction + 1.0) / 6.0,
        cube_part / 6.0,
    ]
    slopes = [
        -0.5 * remain * remain,
        0.5 * (3.0 * square - 4.0 * fraction),
        0.5 * (-3.0 * square + 2.0 * fraction + 1.0),
        0.5 * square,
    ]
    return (values, slopes)


def split_cells(coordinate, offset, cell_count):
    inside = coordinate - offset
    lowest = jnp.clip(jnp.floor(inside).astype(jnp.int32), 0, cell_count - 1)
    return (lowest, inside - lowest.astype(inside.dtype))


def spline_table(lowest, values, table_size, period=None):
    points = lax.broadcasted_iota(jnp.int32, (table_size, lowest.shape[1]), 0)
    lookup = jnp.zeros(points.shape, jnp.float32)
    for spline_term in range(4):
        at = lowest + spline_term
        if period is not None:
            at = jnp.where(at >= period, at - period, at)
        lookup = jnp.where(points == at, values[spline_term], lookup)
    return lookup


def spread_kernel(cells, pad, atoms_ref, base_ref, turn_ref, out_ref, wx_ref, wy_ref, wz_ref, hi_ref, lo_ref):
    cells_x, cells_y, cells_z = cells
    pad_x, pad_y = pad
    atom_total = atoms_ref.shape[1]
    low_x, frac_x = split_cells(atoms_ref[0:1, :], 0.0, cells_x)
    low_y, frac_y = split_cells(atoms_ref[1:2, :], 0.0, cells_y)
    base = base_ref[...]
    low_z, frac_z = split_cells(atoms_ref[2:3, :], base.astype(jnp.float32), cells_z)
    wx_ref[...] = spline_table(low_x, spline_weights(frac_x)[0], pad_x) * atoms_ref[3:4, :]
    wy_ref[...] = spline_table(low_y, spline_weights(frac_y)[0], pad_y)
    turn = turn_ref[...]
    size_z = turn.shape[0]
    table_z = spline_table(base + low_z, spline_weights(frac_z)[0], size_z, size_z)
    waves = jnp.dot(
        turn, table_z, precision=lax.Precision.HIGHEST, preferred_element_type=jnp.float32
    ).T
    high, low = halves(waves)
    wz_ref[:, :size_z] = high
    wz_ref[:, size_z:] = low

    @pl.loop(0, pad_x // rows_group)
    def _(chunk):
        for inner in range(rows_group):
            row = wx_ref[pl.ds(chunk * rows_group + inner, 1), :]
            high, low = halves(row * wy_ref[...])
            hi_ref[pl.ds(inner * pad_y, pad_y), :] = high
            lo_ref[pl.ds(inner * pad_y, pad_y), :] = low
        both = dot(hi_ref[...], wz_ref[...])
        rest = dot(lo_ref[...], wz_ref[:, :size_z])
        total = both[:, :size_z] + both[:, size_z:] + rest
        out_ref[pl.ds(chunk * rows_group, rows_group)] = total.reshape(rows_group, pad_y, size_z)


def gather_kernel(cells, pad, atoms_ref, base_ref, turn_ref, mesh_ref, out_ref, wx_ref, vx_ref, wy_ref, vy_ref, wz_ref, level_ref):
    cells_x, cells_y, cells_z = cells
    pad_x, pad_y = pad
    atom_total = atoms_ref.shape[1]
    low_x, frac_x = split_cells(atoms_ref[0:1, :], 0.0, cells_x)
    low_y, frac_y = split_cells(atoms_ref[1:2, :], 0.0, cells_y)
    base = base_ref[...]
    low_z, frac_z = split_cells(atoms_ref[2:3, :], base.astype(jnp.float32), cells_z)
    values, slopes = spline_weights(frac_x)
    wx_ref[...] = spline_table(low_x, values, pad_x)
    vx_ref[...] = spline_table(low_x, slopes, pad_x)
    values, slopes = spline_weights(frac_y)
    wy_ref[...] = spline_table(low_y, values, pad_y)
    vy_ref[...] = spline_table(low_y, slopes, pad_y)
    values, slopes = spline_weights(frac_z)
    turn = turn_ref[...]
    size_z = turn.shape[0]
    for place, terms in enumerate((values, slopes)):
        table_z = spline_table(base + low_z, terms, size_z, size_z)
        waves = jnp.dot(
            turn, table_z, precision=lax.Precision.HIGHEST, preferred_element_type=jnp.float32
        )
        high, low = halves(waves)
        wz_ref[:size_z, pl.ds(place * atom_total, atom_total)] = high
        wz_ref[size_z:, pl.ds(place * atom_total, atom_total)] = low
    groups = pad_y // 8

    def one_chunk(chunk, sums):
        rows = mesh_ref[pl.ds(chunk * rows_group, rows_group)].reshape(rows_group * pad_y, size_z)
        high, low = halves(rows)
        level_ref[...] = dot(jnp.concatenate([high, high], axis=1), wz_ref[...]) + dot(
            low, wz_ref[:size_z, :]
        )
        first, second, third = sums
        for inner in range(rows_group):
            flat = level_ref[pl.ds(inner * pad_y, pad_y), :atom_total]
            tilt = level_ref[pl.ds(inner * pad_y, pad_y), atom_total:]
            across = wy_ref[...]
            part_x = jnp.sum((across * flat).reshape(groups, 8, atom_total), axis=0)
            part_y = jnp.sum((vy_ref[...] * flat).reshape(groups, 8, atom_total), axis=0)
            part_z = jnp.sum((across * tilt).reshape(groups, 8, atom_total), axis=0)
            weight = wx_ref[pl.ds(chunk * rows_group + inner, 1), :]
            slope = vx_ref[pl.ds(chunk * rows_group + inner, 1), :]
            first = first + slope * part_x
            second = second + weight * part_y
            third = third + weight * part_z
        return (first, second, third)

    zero = jnp.zeros((8, atom_total), jnp.float32)
    sums = lax.fori_loop(0, pad_x // rows_group, one_chunk, (zero, zero, zero))
    factor = -atoms_ref[3:4, :] / spacing
    for place in range(3):
        out_ref[pl.ds(place, 1), :] = factor * jnp.sum(sums[place], axis=0, keepdims=True)


def share_kernel(sizes, atoms_ref, out_ref, send_sem, recv_sem):
    count_x, count_y = sizes
    place_x, place_y = (lax.axis_index("gx"), lax.axis_index("gy"))
    me = place_x * count_y + place_y
    peers = []
    for order in range(1, count_x * count_y):
        peer_x = lax.rem(place_x + order // count_y, count_x)
        peer_y = lax.rem(place_y + order % count_y, count_y)
        peers.append({"gx": peer_x, "gy": peer_y})
    barrier = pltpu.get_barrier_semaphore()
    for peer in peers:
        pl.semaphore_signal(
            barrier, inc=1, device_id=peer, device_id_type=pl.DeviceIdType.MESH
        )
    pl.semaphore_wait(barrier, len(peers))
    copies = [
        pltpu.make_async_remote_copy(
            src_ref=atoms_ref,
            dst_ref=out_ref.at[me],
            send_sem=send_sem.at[order],
            recv_sem=recv_sem.at[order],
            device_id=peer,
            device_id_type=pl.DeviceIdType.MESH,
        )
        for order, peer in enumerate(peers)
    ]
    for copy in copies:
        copy.start()
    out_ref[me] = atoms_ref[...]
    for copy in copies:
        copy.wait()


def shared(atoms, count_x, count_y):
    devices = count_x * count_y
    vmem = pl.BlockSpec(memory_space=pltpu.VMEM)
    flags = pltpu.SemaphoreType.DMA((devices - 1,))
    return pl.pallas_call(
        functools.partial(share_kernel, (count_x, count_y)),
        in_specs=[vmem],
        out_specs=vmem,
        out_shape=jax.ShapeDtypeStruct((devices, *atoms.shape), jnp.float32),
        scratch_shapes=[flags, flags],
        compiler_params=pltpu.CompilerParams(collective_id=0, has_side_effects=True),
        name="share",
    )(atoms)


def depth_rows(table, height, fraction, terms):
    turns = height * table[:, 0:1]
    quarter = GRID_Z // 4
    nearest = jnp.floor(turns * (1.0 / quarter) + 0.5)
    angle = (turns - nearest * quarter) * (2.0 * math.pi / GRID_Z)
    quadrant = nearest - 4.0 * jnp.floor(nearest * 0.25)
    square = angle * angle
    near_cos = 1.0 + square * (
        -0.5 + square * (1.0 / 24.0 + square * (-1.0 / 720.0 + square * (1.0 / 40320.0)))
    )
    near_sin = angle * (
        1.0
        + square
        * (-1.0 / 6.0 + square * (1.0 / 120.0 + square * (-1.0 / 5040.0 + square / 362880.0)))
    )
    odd_turn = (quadrant == 1.0) | (quadrant == 3.0)
    cosine = jnp.where(odd_turn, near_sin, near_cos)
    cosine = jnp.where((quadrant == 1.0) | (quadrant == 2.0), -cosine, cosine)
    sine = jnp.where(odd_turn, near_cos, near_sin)
    sine = jnp.where(quadrant >= 2.0, -sine, sine)
    results = []
    for weights in terms:
        even = sum(table[:, 1 + t : 2 + t] * weights[t] for t in range(4))
        odd = sum(table[:, 5 + t : 6 + t] * weights[t] for t in range(4))
        results.append(cosine * even + sine * odd)
    return results


def mesh_kernel(sizes, cells, pad, atoms_ref, xh_ref, xl_ref, yh_ref, yl_ref, column_ref, row_ref, table_ref, out_ref, mesh_ref, turned_ref, *scratch):
    count_x, count_y = sizes
    cells_x, cells_y = cells
    pad_x, pad_y = pad
    atom_total = atoms_ref.shape[2]
    depth = table_ref.shape[0]
    window = 2 * cells_y
    windows = GRID_Y // window
    lane = lax.broadcasted_iota(jnp.int32, (depth * pad_x, window), 1)
    mesh_ref[...] = jnp.zeros_like(mesh_ref)
    table = table_ref[...]
    per_side = len(scratch) // 2
    banks = (scratch[:per_side], scratch[per_side:])
    for _, _, wy_ref, _, _, _, _, side_ref in banks:
        wy_ref[...] = jnp.zeros_like(wy_ref)
        side_ref[...] = jnp.zeros_like(side_ref)

    def atoms_of(cell, row):
        return atoms_ref[cell, row : row + 1, :]

    def spread_cell(cell, i, j):
        wx_ref, vx_ref, wy_ref, hi_ref, lo_ref, level_ref, stack_ref, side_ref = banks[j % 2]
        low_x, frac_x = split_cells(atoms_of(cell, 0), 0.0, cells_x)
        low_y, frac_y = split_cells(atoms_of(cell, 1), 0.0, cells_y)
        wx_ref[...] = spline_table(low_x, spline_weights(frac_x)[0], pad_x)
        high, low = halves(spline_table(low_y, spline_weights(frac_y)[0], pad_y))
        wy_ref[:pad_y, :] = high
        wy_ref[pl.ds(window, pad_y), :] = low
        height = jnp.floor(atoms_of(cell, 2))
        frac_z = atoms_of(cell, 2) - height
        (deep,) = depth_rows(table, height, frac_z, [spline_weights(frac_z)[0]])
        deep = deep * atoms_of(cell, 3)
        for k in range(depth):
            high, low = halves(deep[k : k + 1, :] * wx_ref[...])
            hi_ref[pl.ds(k * pad_x, pad_x), :] = high
            lo_ref[pl.ds(k * pad_x, pad_x), :] = low
        numbers = (((1,), (1,)), ((), ()))
        both = lax.dot_general(
            hi_ref[...], wy_ref[...], numbers, preferred_element_type=jnp.float32
        )
        rest = lax.dot_general(
            lo_ref[...], wy_ref[:window, :], numbers, preferred_element_type=jnp.float32
        )
        total = both[:, :window] + both[:, window:] + rest
        rows = pl.ds(pl.multiple_of(i * cells_x, 8), pad_x)
        m = j // 2
        if j % 2 == 0:
            mesh_ref[:, rows, pl.ds(m * window, window)] += total.reshape(depth, pad_x, window)
        else:
            total = pltpu.roll(total, cells_y, 1)
            kept = jnp.where(lane >= cells_y, total, 0.0)
            carried = jnp.where(lane < cells_y, total, 0.0)
            after = (m + 1) % windows
            mesh_ref[:, rows, pl.ds(m * window, window)] += kept.reshape(depth, pad_x, window)
            mesh_ref[:, rows, pl.ds(after * window, window)] += carried.reshape(
                depth, pad_x, window
            )

    @pl.loop(0, count_x)
    def _(i):
        for j in range(count_y):
            spread_cell(i * count_y + j, i, j)

    def across(value):
        high, low = halves(value)
        return dot(xh_ref[...], high) + dot(xl_ref[...], high) + dot(xh_ref[...], low)

    def along(value):
        high, low = halves(value)
        return dot(high, yh_ref[...]) + dot(high, yl_ref[...]) + dot(low, yh_ref[...])

    extra = mesh_ref.shape[1] - GRID_X

    @pl.loop(0, depth)
    def _(k):
        mesh_ref[k, :extra, :] += mesh_ref[k, GRID_X:, :]
        waves = along(across(mesh_ref[k, :GRID_X, :]))
        square = column_ref[:, 0:1] + row_ref[0:1, :] + table_ref[pl.ds(k, 1), 9:10]
        scale = column_ref[:, 1:2] * row_ref[1:2, :] * table_ref[pl.ds(k, 1), 10:11]
        green = jnp.where(square > 0.0, scale / jnp.where(square > 0.0, square, 1.0), 0.0)
        plane = across(along(waves * green))
        mesh_ref[k, :GRID_X, :] = plane
        mesh_ref[k, GRID_X:, :] = plane[:extra]
        rolled = pltpu.roll(plane, GRID_Y - cells_y, 1)
        turned_ref[k, :GRID_X, :] = rolled
        turned_ref[k, GRID_X:, :] = rolled[:extra]

    stride = round_up(pad_y, 16)
    groups = pad_x // 8

    def gather_cell(cell, i, j):
        wx_ref, vx_ref, wy_ref, hi_ref, lo_ref, level_ref, stack_ref, side_ref = banks[j % 2]
        low_x, frac_x = split_cells(atoms_of(cell, 0), 0.0, cells_x)
        low_y, frac_y = split_cells(atoms_of(cell, 1), 0.0, cells_y)
        values, slopes = spline_weights(frac_x)
        wx_ref[...] = spline_table(low_x, values, pad_x)
        vx_ref[...] = spline_table(low_x, slopes, pad_x)
        for place, terms in enumerate(spline_weights(frac_y)):
            high, low = halves(spline_table(low_y, terms, stride))
            span = pl.ds(place * atom_total, atom_total)
            side_ref[:stride, span] = high
            side_ref[pl.ds(stride, stride), span] = low
            side_ref[pl.ds(2 * stride, stride), span] = high
        height = jnp.floor(atoms_of(cell, 2))
        frac_z = atoms_of(cell, 2) - height
        deep, steep = depth_rows(table, height, frac_z, spline_weights(frac_z))
        source = mesh_ref if j % 2 == 0 else turned_ref
        rows = pl.ds(pl.multiple_of(i * cells_x, 8), pad_x)
        block = source[:, rows, pl.ds(j // 2 * window, window)].reshape(depth * pad_x, window)
        high = block.astype(jnp.bfloat16).astype(jnp.float32)
        low = block - high
        shifted = pltpu.roll(high, stride, 1)
        stack_ref[:, :window] = jnp.where(lane < stride, high, shifted).astype(jnp.bfloat16)
        stack_ref[:, window:] = jnp.where(
            lane < 2 * stride - window, shifted, pltpu.roll(low, 2 * stride - window, 1)
        ).astype(jnp.bfloat16)
        level_ref[...] = dot(stack_ref[...], side_ref[...])
        zero = jnp.zeros((8, atom_total), jnp.float32)
        first, second, third = (zero, zero, zero)
        for k in range(depth):
            flat = level_ref[pl.ds(k * pad_x, pad_x), :atom_total]
            tilt = level_ref[pl.ds(k * pad_x, pad_x), atom_total:]
            weight = wx_ref[...]
            part_x = jnp.sum((vx_ref[...] * flat).reshape(groups, 8, atom_total), axis=0)
            part_y = jnp.sum((weight * tilt).reshape(groups, 8, atom_total), axis=0)
            part_z = jnp.sum((weight * flat).reshape(groups, 8, atom_total), axis=0)
            first = first + deep[k : k + 1, :] * part_x
            second = second + deep[k : k + 1, :] * part_y
            third = third + steep[k : k + 1, :] * part_z
        for place, value in enumerate((first, second, third)):
            out_ref[cell, pl.ds(place, 1), :] = jnp.sum(value, axis=0, keepdims=True)
        out_ref[cell, 3:4, :] = jnp.zeros((1, atom_total), jnp.float32)

    @pl.loop(0, count_x)
    def _(i):
        for j in range(count_y):
            gather_cell(i * count_y + j, i, j)


def green_table(period):
    index = np.arange(period)
    signed = np.where(index <= period // 2, index, index - period) / (period * spacing)
    modulus = ((2.0 + np.cos(index * (2.0 * np.pi / period))) / 3.0) ** 2
    square = signed * signed
    return np.stack([square, np.exp(-((np.pi / ewald_split) ** 2) * square) / modulus]).astype(
        np.float32
    )


def green_factors(index, period):
    signed = jnp.where(index <= period // 2, index, index - period).astype(jnp.float32) / (
        period * spacing
    )
    modulus = ((2.0 + jnp.cos(index.astype(jnp.float32) * (2.0 * jnp.pi / period))) / 3.0) ** 2
    square = signed * signed
    return jnp.stack([square, jnp.exp(-((jnp.pi / ewald_split) ** 2) * square) / modulus])


def one_cluster(own_rows, partner):
    offsets = (own_rows[:3, :, None] - partner[:3, None, :]) * spacing
    dist_square = jnp.sum(offsets * offsets, axis=0)
    soft_square = dist_square + soft_core
    soft_dist = jnp.sqrt(soft_square)
    scaled = ewald_split * soft_dist
    strength = (
        jax.scipy.special.erfc(scaled) / soft_dist
        + ewald_split * root_factor * jnp.exp(-scaled * scaled)
    ) / soft_square
    cutoff_taper = jnp.where(
        dist_square < cutoff * cutoff, (1.0 - dist_square / (cutoff * cutoff)) ** 2, 0.0
    )
    weight = partner[3][None, :] * strength * cutoff_taper
    return own_rows[3] * jnp.sum(weight[None] * offsets, axis=2)


def far_by_planes(gathered, own_charge, count_x, count_y, cells_x, cells_y):
    devices = count_x * count_y
    place = lax.axis_index("gx") * count_y + lax.axis_index("gy")
    depth = GRID_Z // devices
    atom_total = gathered.shape[2]
    pad_x = round_up(cells_x + 3, 8)
    pad_y = round_up(cells_y + 3, 8)
    window = 2 * cells_y
    turn_x = halves(jnp.asarray(hartley(GRID_X)))
    turn_y = halves(jnp.asarray(hartley(GRID_Y)))
    volume = GRID_X * GRID_Y * GRID_Z * spacing**3
    column = jnp.asarray(green_table(GRID_X).T)
    row = jnp.asarray(green_table(GRID_Y))
    every_k = np.arange(GRID_Z)
    taps = np.outer(every_k, np.arange(4)) * (2.0 * np.pi / GRID_Z)
    square, scale = green_table(GRID_Z)
    table = np.concatenate(
        [
            every_k[:, None],
            np.cos(taps) + np.sin(taps),
            np.cos(taps) - np.sin(taps),
            square[:, None],
            scale[:, None] / (np.pi * volume),
        ],
        axis=1,
    ).astype(np.float32)
    table = lax.dynamic_slice_in_dim(jnp.asarray(table), place * depth, depth, axis=0)
    vmem = pl.BlockSpec(memory_space=pltpu.VMEM)
    rows = GRID_X + pad_x - cells_x
    bank = [
        pltpu.VMEM((pad_x, atom_total), jnp.float32),
        pltpu.VMEM((pad_x, atom_total), jnp.float32),
        pltpu.VMEM((2 * window, atom_total), jnp.bfloat16),
        pltpu.VMEM((depth * pad_x, atom_total), jnp.bfloat16),
        pltpu.VMEM((depth * pad_x, atom_total), jnp.bfloat16),
        pltpu.VMEM((depth * pad_x, 2 * atom_total), jnp.float32),
        pltpu.VMEM((depth * pad_x, 2 * window), jnp.bfloat16),
        pltpu.VMEM((2 * window, 2 * atom_total), jnp.bfloat16),
    ]
    partial = pl.pallas_call(
        functools.partial(mesh_kernel, (count_x, count_y), (cells_x, cells_y), (pad_x, pad_y)),
        in_specs=[vmem] * 8,
        out_specs=vmem,
        out_shape=jax.ShapeDtypeStruct((devices, 4, atom_total), jnp.float32),
        scratch_shapes=[pltpu.VMEM((depth, rows, GRID_Y), jnp.float32)] * 2 + 2 * bank,
        name="mesh",
    )(gathered, *turn_x, *turn_y, column, row, table)
    parts = lax.all_to_all(partial, ("gx", "gy"), split_axis=0, concat_axis=0, tiled=True)
    total = jnp.sum(parts, axis=0)[:3]
    return total * (-own_charge / spacing)


def convolved_by_lines(charge_mesh, count_x, count_y):
    turn_x = jnp.asarray(hartley(GRID_X))
    turn_y = jnp.asarray(hartley(GRID_Y))
    product = functools.partial(
        jnp.einsum, precision=lax.Precision.HIGHEST, preferred_element_type=jnp.float32
    )
    exchange = functools.partial(lax.all_to_all, tiled=True)
    lines = exchange(charge_mesh, "gx", split_axis=2, concat_axis=0)
    lines = product("xyk,xu->uyk", lines, turn_x)
    lines = exchange(lines, "gy", split_axis=0, concat_axis=1)
    lines = product("uyk,yv->uvk", lines, turn_y)
    wide, _, depth = lines.shape
    start_x = lax.axis_index("gy") * wide
    start_z = lax.axis_index("gx") * depth
    volume = GRID_X * GRID_Y * GRID_Z * spacing**3
    fx = green_factors(start_x + jnp.arange(wide, dtype=jnp.int32), GRID_X)
    fy = green_factors(jnp.arange(GRID_Y, dtype=jnp.int32), GRID_Y)
    fz = green_factors(start_z + jnp.arange(depth, dtype=jnp.int32), GRID_Z)
    square = fx[0][:, None, None] + fy[0][:, None] + fz[0]
    scale = fx[1][:, None, None] * fy[1][:, None] * fz[1] / (math.pi * volume)
    lines = lines * jnp.where(square > 0.0, scale / jnp.where(square > 0.0, square, 1.0), 0.0)
    lines = product("uvk,vy->uyk", lines, turn_y)
    lines = exchange(lines, "gy", split_axis=1, concat_axis=0)
    lines = product("uyk,ux->xyk", lines, turn_x)
    return exchange(lines, "gx", split_axis=0, concat_axis=2)


def far_by_lines(atoms, base, count_x, count_y, cells_x, cells_y, cells_z):
    atom_total = atoms.shape[1]
    cells = (cells_x, cells_y, cells_z)
    pad = (round_up(cells_x + 3, rows_group), round_up(cells_y + 3, 8))
    pad_x, pad_y = pad
    turn_z = jnp.asarray(hartley(GRID_Z))
    spread = pl.pallas_call(
        functools.partial(spread_kernel, cells, pad),
        out_shape=jax.ShapeDtypeStruct((pad_x, pad_y, GRID_Z), jnp.float32),
        scratch_shapes=[
            pltpu.VMEM((pad_x, atom_total), jnp.float32),
            pltpu.VMEM((pad_y, atom_total), jnp.float32),
            pltpu.VMEM((atom_total, 2 * GRID_Z), jnp.bfloat16),
            pltpu.VMEM((rows_group * pad_y, atom_total), jnp.bfloat16),
            pltpu.VMEM((rows_group * pad_y, atom_total), jnp.bfloat16),
        ],
        name="spread",
    )(atoms, base, turn_z)

    from_x = moved(spread[cells_x : cells_x + 3, :cells_y], 1, 0)
    from_y = moved(spread[:cells_x, cells_y : cells_y + 3], 0, 1)
    from_both = moved(spread[cells_x : cells_x + 3, cells_y : cells_y + 3], 1, 1)
    charge_mesh = (
        spread[:cells_x, :cells_y]
        .at[:3]
        .add(from_x)
        .at[:, :3]
        .add(from_y)
        .at[:3, :3]
        .add(from_both)
    )
    potential = convolved_by_lines(charge_mesh, count_x, count_y)
    upper_x = moved(potential[:3], -1, 0)
    upper_y = moved(potential[:, :3], 0, -1)
    upper_both = moved(potential[:3, :3], -1, -1)
    wider = jnp.concatenate(
        [
            jnp.concatenate([potential, upper_x], axis=0),
            jnp.concatenate([upper_y, upper_both], axis=0),
        ],
        axis=1,
    )
    wider = jnp.pad(wider, ((0, pad_x - cells_x - 3), (0, pad_y - cells_y - 3), (0, 0)))
    return pl.pallas_call(
        functools.partial(gather_kernel, cells, pad),
        out_shape=jax.ShapeDtypeStruct((3, atom_total), jnp.float32),
        scratch_shapes=[
            pltpu.VMEM((pad_x, atom_total), jnp.float32),
            pltpu.VMEM((pad_x, atom_total), jnp.float32),
            pltpu.VMEM((pad_y, atom_total), jnp.float32),
            pltpu.VMEM((pad_y, atom_total), jnp.float32),
            pltpu.VMEM((2 * GRID_Z, 2 * atom_total), jnp.bfloat16),
            pltpu.VMEM((rows_group * pad_y, 2 * atom_total), jnp.float32),
        ],
        name="gather",
    )(atoms, base, turn_z, wider)


def local(positions, charges, pair_lists, slab_dest, atom_counts):
    count_x = lax.axis_size("gx")
    count_y = lax.axis_size("gy")
    devices = count_x * count_y
    atom_total = positions.shape[3]
    clusters = pair_lists.shape[2]
    cluster_size = atom_total // clusters
    blocks = slab_dest.shape[2]
    block_size = atom_total // blocks
    cells_x = GRID_X // count_x
    cells_y = GRID_Y // count_y
    cells_z = GRID_Z // count_y
    living = jnp.arange(atom_total, dtype=jnp.int32) < atom_counts[0, 0]
    charge = jnp.where(living, charges[0, 0], 0.0)
    packed = jnp.concatenate([positions, charge[None, None, None, :]], axis=0)
    atoms = packed.reshape(4, atom_total)

    base = jnp.broadcast_to(
        (slab_dest[0, 0] * cells_z)[:, None], (blocks, block_size)
    ).reshape(1, atom_total)
    by_planes = GRID_Z % devices == 0 and cells_y == 64 and cells_x % 8 == 0
    if by_planes:
        gathered = shared(atoms, count_x, count_y)
    else:
        gathered = lax.all_gather(atoms, ("gx", "gy"), axis=0, tiled=False)
    if by_planes:
        far_part = far_by_planes(gathered, charge, count_x, count_y, cells_x, cells_y)
    else:
        far_part = far_by_lines(atoms, base, count_x, count_y, cells_x, cells_y, cells_z)

    chosen = pair_lists[0, 0]
    beside = chosen // clusters
    step_x, step_y = (beside // 3 - 1, beside % 3 - 1)
    at_x = (lax.axis_index("gx") + step_x + count_x) % count_x
    at_y = (lax.axis_index("gy") + step_y + count_y) % count_y
    number = (at_x * count_y + at_y) * clusters + chosen % clusters
    pick = (number[:, :, None] == jnp.arange(devices * clusters, dtype=jnp.int32)).astype(
        jnp.float32
    )
    pool = gathered[:, :4].reshape(devices, 4, clusters, cluster_size)
    pool = jnp.transpose(pool, (1, 0, 2, 3)).reshape(4, devices * clusters, cluster_size)
    partners = jnp.einsum(
        "cln,fnk->cflk",
        pick,
        pool,
        precision=lax.Precision.HIGHEST,
        preferred_element_type=jnp.float32,
    )
    shift_x = (step_x * cells_x).astype(jnp.float32)
    shift_y = (step_y * cells_y).astype(jnp.float32)
    flat = jnp.zeros_like(shift_x)
    shift = jnp.stack([shift_x, shift_y, flat, flat], axis=1)
    partners = (partners + shift[:, :, :, None]).reshape(clusters, 4, -1)
    own = packed.reshape(4, clusters, cluster_size)
    pair_part = jnp.stack(
        [one_cluster(own[:, c], partners[c]) for c in range(clusters)], axis=1
    )
    short_forces = pair_part.reshape(3, 1, 1, atom_total)
    return (short_forces, far_part.reshape(3, 1, 1, atom_total))


def solution(mesh):
    return jax.shard_map(
        local,
        mesh=mesh,
        in_specs=(
            P(None, ("rep", "gx"), "gy", None),
            P(("rep", "gx"), "gy", None),
            P(("rep", "gx"), "gy", None, None),
            P(("rep", "gx"), "gy", None),
            P(("rep", "gx"), "gy"),
        ),
        out_specs=(P(None, ("rep", "gx"), "gy", None), P(None, ("rep", "gx"), "gy", None)),
        check_vma=False,
    )
```
